256 devices in a mesh: space: 64 (over x, z, core), tpair: 4 (over y).
Axes of the slice: x: 4, y: 4, z: 8, core: 2. Of those that a mesh axis runs over, the one named last changes fastest.
Arguments:
- eigvecs: bfloat16 [4, 2, 3, 64, 8192], P('tpair', None, None, None, 'space'), may hold values from -6 to 6
- momenta: int32 [8, 3], replicated, may hold values from -2 to 2
- perams: bfloat16 [4, 4, 16, 2, 4096], P('tpair'), may hold values from -0.5 to 0.5
- sources: int32 [4], replicated, may hold values from 0 to 3, each once
- spins: int32 [2, 3, 2], replicated, may hold values from 0 to 3
Outputs:
- baryon: float32 [4, 4, 2, 512, 2, 4096], P('tpair', None, None, 'space')
The draws below stay inside these ranges and needn't reach their ends.
Inputs may be any that keep to these rules, and one draw needn't show every extreme that they name: The entries of sources are distinct.
All inputs are finite; a program needn't handle non-finite values.
Results may differ from the reference program's by a relative error of at most 0.0064.
Values may be sent and summed in bfloat16 or wider, within the bound.
A program may use at most 128 MiB of HBM per device.

```python
import jax
import jax.numpy as jnp
import numpy as np
from jax import lax

NVEC = 64
MOM = 8
LEXT = 64
NCOMB = 2
NSRC = 4
SITES_DEV = 128
NT = 4
SITES = 8192
N_SPACE = 64


def touch_ends(array, stream_key, low, top_value):
    extent = array.shape
    place = [jax.random.randint(jax.random.fold_in(stream_key, axis), (), 0, extent[axis]) for axis in range(len(extent))]
    array = array.at[tuple(place)].set(low)
    longest = extent.index(max(extent))
    place[longest] = (place[longest] + 1) % extent[longest]
    return array.at[tuple(place)].set(top_value)


def steps_of(key, extent, shards, smallest, high):
    factor_of, own = 1.0, jax.random.fold_in(key, 6)
    for dim, blocks in shards:
        heights = jnp.exp(jax.random.uniform(jax.random.fold_in(own, dim), (blocks,), jnp.float32, smallest / len(shards), high / len(shards)))
        factor_of = factor_of * jnp.repeat(heights, extent[dim] // blocks).reshape([-1 if axis == dim else 1 for axis in range(len(extent))])
    return factor_of


def centred(stream_key, extent, deviation, limit, shards=(), kind=jnp.bfloat16):
    values = deviation * jax.random.normal(stream_key, extent, jnp.float32)
    if shards:
        values = values * steps_of(stream_key, extent, shards, -0.22, 0.18)
    return jnp.clip(values, -limit, limit).astype(kind)


def setup_inputs(seed: int = 0) -> dict:
    streams_of = jax.random.split(jax.random.key(seed), 6)
    eigvecs = centred(streams_of[0], (NT, 2, 3, NVEC, SITES), 1.0, 6.0, ((0, 4), (4, 64)))
    momenta = touch_ends(jax.random.randint(streams_of[1], (MOM, 3), -2, 3), jax.random.fold_in(streams_of[1], 1), -2, 2).astype(jnp.int32)
    perams = centred(streams_of[2], (NT, NT, 16, 2, NVEC * NVEC), (2 * NVEC) ** -0.5, 0.5, ((0, 4),))
    sources = jax.random.permutation(streams_of[3], NT).astype(jnp.int32)
    spins = touch_ends(jax.random.randint(streams_of[4], (NCOMB, 3, 2), 0, 4), jax.random.fold_in(streams_of[4], 1), 0, 3).astype(jnp.int32)
    return dict(eigvecs=eigvecs, momenta=momenta, perams=perams, sources=sources, spins=spins)


TWO_PI = 6.283185307179586

def pair_tables(vectors):
    upper_rows, upper_cols = np.triu_indices(vectors, 1)
    total_pairs = vectors * vectors // 2
    left_index = np.zeros(total_pairs, np.int32)
    right_index = np.zeros(total_pairs, np.int32)
    left_index[:upper_rows.size] = upper_rows
    right_index[:upper_rows.size] = upper_cols
    position = np.zeros(vectors * vectors, np.int32)
    sign_table = np.zeros(vectors * vectors, np.float32)
    slot_ids = np.arange(upper_rows.size, dtype=np.int32)
    position[upper_rows * vectors + upper_cols] = slot_ids
    sign_table[upper_rows * vectors + upper_cols] = 1.0
    position[upper_cols * vectors + upper_rows] = slot_ids
    sign_table[upper_cols * vectors + upper_rows] = -1.0
    return (left_index, right_index, position, sign_table)

def cross_columns(left_vec, right_vec):
    left_f = left_vec.astype(jnp.float32)
    right_f = right_vec.astype(jnp.float32)
    pieces = []
    for colour in range(3):
        next_one = (colour + 1) % 3
        after_one = (colour + 2) % 3
        real_part = left_f[:, 0, next_one] * right_f[:, 0, after_one] - left_f[:, 1, next_one] * right_f[:, 1, after_one] - (left_f[:, 0, after_one] * right_f[:, 0, next_one] - left_f[:, 1, after_one] * right_f[:, 1, next_one])
        imag_part = left_f[:, 0, next_one] * right_f[:, 1, after_one] + left_f[:, 1, next_one] * right_f[:, 0, after_one] - (left_f[:, 0, after_one] * right_f[:, 1, next_one] + left_f[:, 1, after_one] * right_f[:, 0, next_one])
        pieces.append(jnp.stack([real_part, imag_part], axis=1))
    return jnp.stack(pieces, axis=2).astype(jnp.bfloat16)

def projected_left(block_vecs, momenta, offset, total_sites):
    site_count = block_vecs.shape[-1]
    site_ids = offset + jnp.arange(site_count, dtype=jnp.int32)
    coords = jnp.stack([site_ids % LEXT, site_ids // LEXT % LEXT, site_ids // (LEXT * LEXT)])
    turns = jnp.mod(lax.optimization_barrier(jnp.sum(momenta[:, :, None] * coords[None, :, :], axis=1)), LEXT)
    angle = turns.astype(jnp.float32) * (TWO_PI / LEXT)
    factor = lax.rsqrt(jnp.float32(24.0 * total_sites))
    cosine = (jnp.cos(angle) * factor)[:, None, None, :]
    sine = (jnp.sin(angle) * factor)[:, None, None, :]
    vfloat = block_vecs.astype(jnp.float32)
    left_real = cosine * vfloat[0][None] + sine * vfloat[1][None]
    left_imag = cosine * vfloat[1][None] - sine * vfloat[0][None]
    upper_half = jnp.stack([left_real, left_imag], axis=0)
    lower_half = jnp.stack([-left_imag, left_real], axis=0)
    stacked = jnp.stack([upper_half, lower_half], axis=0)
    mom_count = momenta.shape[0]
    vectors = block_vecs.shape[2]
    stacked = jnp.transpose(stacked, (0, 3, 5, 1, 2, 4)).reshape(6 * site_count, 2 * mom_count * vectors)
    return stacked.astype(jnp.bfloat16)

def complex_blocks(blocks):
    tau_real = blocks[..., 0, :, :]
    tau_imag = blocks[..., 1, :, :]
    upper_half = jnp.stack([tau_real, tau_imag], axis=-2)
    lower_half = jnp.stack([-tau_imag, tau_real], axis=-2)
    return jnp.stack([upper_half, lower_half], axis=-4)

def select_blocks(sink_perams, sources, spins, vectors):
    count_times = sink_perams.shape[0]
    pick_time = (sources[:, None] == jnp.arange(count_times, dtype=jnp.int32)[None, :]).astype(jnp.float32)
    spin_code = spins[:, :, 0] * 4 + spins[:, :, 1]
    pick_spin = (spin_code[:, :, None] == jnp.arange(16, dtype=jnp.int32)).astype(jnp.float32)
    chosen = jnp.einsum('st,cqa,taxy->scqxy', pick_time, pick_spin, sink_perams.astype(jnp.float32))
    return chosen.astype(jnp.bfloat16).reshape(sources.shape[0] * spins.shape[0], 3, 2, vectors, vectors)

def reference(eigvecs, momenta, perams, sources, spins):
    left_index, right_index, position, sign_table = pair_tables(NVEC)
    signs = jnp.asarray(sign_table).astype(jnp.bfloat16)
    outputs = []
    for sink in range(NT):
        vecs = eigvecs[sink]

        def block(running, offset):
            block_vecs = lax.dynamic_slice_in_dim(vecs, offset, SITES_DEV, 3)
            turned = jnp.transpose(block_vecs, (2, 0, 1, 3))
            columns = cross_columns(turned[left_index], turned[right_index]).reshape(left_index.size, -1)
            projected = projected_left(block_vecs, momenta, offset, SITES)
            return (running + jnp.dot(columns, projected, preferred_element_type=jnp.float32), None)
        starts = jnp.arange(N_SPACE, dtype=jnp.int32) * SITES_DEV
        empty_sum = jnp.zeros((left_index.size, 2 * MOM * NVEC), jnp.float32)
        summed, _ = lax.scan(block, empty_sum, starts)
        rounded = summed.astype(jnp.bfloat16)
        rounded = (rounded[position] * signs[:, None]).reshape(NVEC * NVEC, 2, MOM, NVEC)
        blocks = select_blocks(perams[:, sink], sources, spins, NVEC)
        ymats = complex_blocks(blocks).astype(jnp.float32)
        spread = jnp.einsum('cwmi,swiox->somxc', rounded.astype(jnp.float32), ymats[:, 0]).astype(jnp.bfloat16)
        count_sc = spread.shape[0]
        spread = spread.reshape(count_sc, 2, MOM * NVEC, NVEC, NVEC).astype(jnp.float32)
        middle = jnp.einsum('swpjk,swkox->spjox', spread, ymats[:, 2]).astype(jnp.bfloat16)
        result = jnp.einsum('spjwk,swjox->spoxk', middle.astype(jnp.float32), ymats[:, 1])
        outputs.append(result.reshape(NSRC, NCOMB, MOM * NVEC, 2, NVEC * NVEC))
    return jnp.stack(outputs, axis=0)
```

```python
import jax
import jax.numpy as jnp
from jax import lax
from jax.experimental import pallas as pl
from jax.experimental.pallas import tpu as pltpu
from jax.sharding import PartitionSpec as P

LEXT = 64
TWO_PI = 6.283185307179586
MESH = pl.DeviceIdType.MESH

NX, NZ, NC = 4, 8, 2
NY = 4
HALF = NZ // 2


def place():
    index = lax.axis_index("space")
    return index // (NZ * NC), (index // NC) % NZ, index % NC


def at_space(x, z, c):
    return {"space": (x * NZ + z) * NC + c}


def elemental_kernel(
    vec_ref, mom_ref, per_ref, elem_ref, arrived_ref,
    cosines, sines, fields, vfloat, left, right, total, outbox, inbox, chunk, all_chunks,
    ring_send, ring_recv, pair_send, pair_recv, sum_send, sum_recv,
    share_send, share_recv, swap_send, swap_recv, per_send, per_recv, per_own, own_sem,
):
    x, z, c = place()
    y = lax.axis_index("tpair")
    zhalf, zz = z // HALF, z % HALF
    slot_q = zz * NC + c
    on_right = at_space(x, (z + 1) % NZ, c)
    on_left = at_space(x, (z + NZ - 1) % NZ, c)
    partner = at_space(x, z, 1 - c)
    across = [at_space((x + step) % NX, z, c) for step in range(1, NX)]
    along = [at_space(x, zhalf * HALF + (zz + step) % HALF, c) for step in range(1, HALF)]
    sinks = [{"tpair": (y + step) % NY} for step in range(1, NY)]

    barrier = pltpu.get_barrier_semaphore()
    greeted = [on_right, on_left, partner] + across + along + sinks
    for target in greeted:
        pl.semaphore_signal(barrier, inc=1, device_id=target, device_id_type=MESH)
    own = pltpu.make_async_copy(vec_ref, fields.at[0, 0], own_sem)
    own.start()
    pl.semaphore_wait(barrier, len(greeted))
    own.wait()

    def ring_copy(rel, colour, rightward):
        there = (rel + NZ - 1) % NZ if rightward else (rel + 1) % NZ
        return pltpu.make_async_remote_copy(
            src_ref=fields.at[0, rel, :, colour],
            dst_ref=fields.at[0, there, :, colour],
            send_sem=ring_send.at[there, colour],
            recv_sem=ring_recv.at[there, colour],
            device_id=on_right if rightward else on_left,
            device_id_type=MESH,
        )

    def ring_arrival(rel, colour):
        return pltpu.make_async_remote_copy(
            src_ref=fields.at[0, rel, :, colour],
            dst_ref=fields.at[0, rel, :, colour],
            send_sem=ring_send.at[rel, colour],
            recv_sem=ring_recv.at[rel, colour],
            device_id=on_right,
            device_id_type=MESH,
        )

    def pair_copy(rel, colour):
        return pltpu.make_async_remote_copy(
            src_ref=fields.at[0, rel, :, colour],
            dst_ref=fields.at[1, rel, :, colour],
            send_sem=pair_send.at[rel, colour],
            recv_sem=pair_recv.at[rel, colour],
            device_id=partner,
            device_id_type=MESH,
        )

    for colour in range(3):
        ring_copy(0, colour, True).start()
        ring_copy(0, colour, False).start()
        pair_copy(0, colour).start()

    per_copies = []
    for step in range(1, NY):
        other = (y + step) % NY
        copy = pltpu.make_async_remote_copy(
            src_ref=per_ref.at[other],
            dst_ref=arrived_ref.at[y],
            send_sem=per_send.at[step - 1],
            recv_sem=per_recv.at[step - 1],
            device_id=sinks[step - 1],
            device_id_type=MESH,
        )
        copy.start()
        per_copies.append(copy)
    per_local = pltpu.make_async_copy(per_ref.at[y], arrived_ref.at[y], per_own)
    per_local.start()

    def relay(place_in_order):
        rel = jnp.where(place_in_order % 2 == 1, NZ - (place_in_order + 1) // 2, place_in_order // 2)
        for colour in range(3):
            ring_arrival(rel, colour).wait_recv()

            @pl.when((place_in_order % 2 == 1) & (place_in_order < 7))
            def _():
                ring_copy(rel, colour, True).start()

            @pl.when((place_in_order % 2 == 0) & (place_in_order < 6))
            def _():
                ring_copy(rel, colour, False).start()

            pair_copy(rel, colour).start()

    row = lax.broadcasted_iota(jnp.int32, (NC * NZ, 128), 0)
    lane = lax.broadcasted_iota(jnp.int32, (NC * NZ, 128), 1)
    core = jnp.where(row < NZ, c, 1 - c)
    sites = ((x * NZ + ((z + row) & (NZ - 1))) * NC + core) * 128 + lane
    xs, ys, zs = sites & (LEXT - 1), (sites >> 6) & (LEXT - 1), sites >> 12
    factor = lax.rsqrt(jnp.float32(24.0 * 128 * NX * NZ * NC))
    for mom in range(4):
        mine = 2 * mom + zhalf
        turns = mom_ref[mine, 0] * xs + mom_ref[mine, 1] * ys + mom_ref[mine, 2] * zs
        angle = (turns & (LEXT - 1)).astype(jnp.float32) * (TWO_PI / LEXT)
        cosines[mom] = jnp.cos(angle) * factor
        sines[mom] = jnp.sin(angle) * factor

    total[...] = jnp.zeros_like(total)

    def contract(core_slot, rel):
        for part in range(2):
            for colour in range(3):
                values = fields[core_slot, rel, part, colour].astype(jnp.float32)
                vfloat[part, colour, 0:64] = values
                vfloat[part, colour, 64:128] = values
        for colour in range(3):
            nxt, aft = (colour + 1) % 3, (colour + 2) % 3
            for odd in range(2):
                rows = pl.ds(odd, 32, stride=2)
                lrn, lin = vfloat[0, nxt, rows], vfloat[1, nxt, rows]
                lra, lia = vfloat[0, aft, rows], vfloat[1, aft, rows]
                for group in range(4):
                    rows = pl.ds(1 + slot_q + 8 * group + odd, 32, stride=2)
                    rrn, rin = vfloat[0, nxt, rows], vfloat[1, nxt, rows]
                    rra, ria = vfloat[0, aft, rows], vfloat[1, aft, rows]
                    real = lrn * rra - lin * ria - (lra * rrn - lia * rin)
                    imag = lrn * ria + lin * rra - (lra * rin + lia * rrn)
                    where = pl.ds(group * 64 + odd * 32, 32)
                    left[where, colour * 128 : (colour + 1) * 128] = real.astype(jnp.bfloat16)
                    left[where, (3 + colour) * 128 : (4 + colour) * 128] = imag.astype(jnp.bfloat16)
        at = pl.ds(core_slot * NZ + rel, 1)
        for colour in range(3):
            for odd in range(2):
                rows = pl.ds(odd, 32, stride=2)
                vr, vi = vfloat[0, colour, rows], vfloat[1, colour, rows]
                for mom in range(4):
                    cosine, sine = cosines[mom, at, :], sines[mom, at, :]
                    pr = (cosine * vr + sine * vi).astype(jnp.bfloat16)
                    pi = (cosine * vi - sine * vr).astype(jnp.bfloat16)
                    upper, lower = pl.ds(mom * 128 + odd * 32, 32), pl.ds(mom * 128 + 64 + odd * 32, 32)
                    first, second = pl.ds(colour * 128, 128), pl.ds((3 + colour) * 128, 128)
                    right[upper, first] = pr
                    right[upper, second] = -pi
                    right[lower, first] = pi
                    right[lower, second] = pr
        product = lax.dot_general(
            left[...], right[...], (((1,), (1,)), ((), ())), preferred_element_type=jnp.float32
        )
        for mom in range(4):
            total[mom] += product[:, mom * 128 : (mom + 1) * 128]

    relay(1)
    relay(2)

    def body(n, carry):
        rel = jnp.where(n % 2 == 1, NZ - (n + 1) // 2, n // 2)

        @pl.when((n >= 1) & (n < 6))
        def _():
            relay(n + 2)

        contract(0, rel)
        for colour in range(3):
            pair_copy(rel, colour).wait_recv()
        contract(1, rel)
        return carry

    lax.fori_loop(0, NZ, body, 0)

    sum_copies = []
    for step in (2, 1, 3):
        outbox[step - 1] = total[(x + step) % NX].astype(jnp.bfloat16)
        copy = pltpu.make_async_remote_copy(
            src_ref=outbox.at[step - 1],
            dst_ref=inbox.at[step - 1],
            send_sem=sum_send.at[step - 1],
            recv_sem=sum_recv.at[step - 1],
            device_id=across[step - 1],
            device_id_type=MESH,
        )
        copy.start()
        sum_copies.append(copy)
    for copy in sum_copies:
        copy.wait_recv()
    summed = total[x]
    for step in range(3):
        summed = summed + inbox[step].astype(jnp.float32)
    chunk[...] = summed.astype(jnp.bfloat16)

    def swap_copy(source, step):
        owner = (zz + NX - step) % HALF
        return pltpu.make_async_remote_copy(
            src_ref=source,
            dst_ref=all_chunks.at[owner * NC + c],
            send_sem=swap_send.at[step],
            recv_sem=swap_recv.at[step],
            device_id=partner,
            device_id_type=MESH,
        )

    share_copies = []
    for step in (3, 2, 1):
        copy = pltpu.make_async_remote_copy(
            src_ref=chunk,
            dst_ref=all_chunks.at[slot_q],
            send_sem=share_send.at[step - 1],
            recv_sem=share_recv.at[step - 1],
            device_id=along[step - 1],
            device_id_type=MESH,
        )
        copy.start()
        share_copies.append((step, copy))
    swap_copies = [swap_copy(chunk, 0)]
    swap_copies[0].start()
    elem_ref[slot_q] = chunk[...]
    for step, copy in reversed(share_copies):
        owner = (zz + HALF - step) % HALF
        arrival = pltpu.make_async_remote_copy(
            src_ref=chunk,
            dst_ref=all_chunks.at[owner * NC + c],
            send_sem=share_send.at[step - 1],
            recv_sem=share_recv.at[step - 1],
            device_id=along[step - 1],
            device_id_type=MESH,
        )
        arrival.wait_recv()
        onward = swap_copy(all_chunks.at[owner * NC + c], step)
        onward.start()
        swap_copies.append(onward)
        elem_ref[owner * NC + c] = all_chunks[owner * NC + c]
    for step in range(HALF):
        owner = (zz + HALF - step) % HALF
        theirs = owner * NC + 1 - c
        pltpu.make_async_remote_copy(
            src_ref=chunk,
            dst_ref=all_chunks.at[theirs],
            send_sem=swap_send.at[step],
            recv_sem=swap_recv.at[step],
            device_id=partner,
            device_id_type=MESH,
        ).wait_recv()
        elem_ref[theirs] = all_chunks[theirs]

    for rel in range(NZ):
        for colour in range(3):
            if rel in (7, 6, 5, 4):
                ring_copy((rel + 1) % NZ, colour, True).wait_send()
            elif rel:
                ring_copy(rel - 1, colour, False).wait_send()
            pair_copy(rel, colour).wait_send()
    for copy in sum_copies:
        copy.wait_send()
    for _, copy in share_copies:
        copy.wait_send()
    for copy in swap_copies:
        copy.wait_send()
    per_local.wait()
    for step, copy in enumerate(per_copies, 1):
        copy.wait_send()
        pltpu.make_async_remote_copy(
            src_ref=per_ref.at[y],
            dst_ref=arrived_ref.at[(y + NY - step) % NY],
            send_sem=per_send.at[step - 1],
            recv_sem=per_recv.at[step - 1],
            device_id=sinks[step - 1],
            device_id_type=MESH,
        ).wait_recv()


def elementals(vecs, momenta, perams):
    vmem = pl.BlockSpec(memory_space=pltpu.VMEM)
    anyspace = pl.BlockSpec(memory_space=pl.ANY)
    dma, bf16, f32 = pltpu.SemaphoreType.DMA, jnp.bfloat16, jnp.float32
    return pl.pallas_call(
        elemental_kernel,
        out_shape=(
            jax.ShapeDtypeStruct((8, 256, 128), bf16),
            jax.ShapeDtypeStruct(perams.shape, bf16),
        ),
        in_specs=[vmem, pl.BlockSpec(memory_space=pltpu.SMEM), anyspace],
        out_specs=(vmem, anyspace),
        scratch_shapes=[
            pltpu.VMEM((4, NC * NZ, 128), f32),
            pltpu.VMEM((4, NC * NZ, 128), f32),
            pltpu.VMEM((NC, NZ, 2, 3, 64, 128), bf16),
            pltpu.VMEM((2, 3, 128, 128), f32),
            pltpu.VMEM((256, 768), bf16),
            pltpu.VMEM((512, 768), bf16),
            pltpu.VMEM((4, 256, 128), f32),
            pltpu.VMEM((3, 256, 128), bf16),
            pltpu.VMEM((3, 256, 128), bf16),
            pltpu.VMEM((256, 128), bf16),
            pltpu.VMEM((8, 256, 128), bf16),
            dma((NZ, 3)), dma((NZ, 3)), dma((NZ, 3)), dma((NZ, 3)),
            dma((3,)), dma((3,)), dma((3,)), dma((3,)), dma((4,)), dma((4,)),
            dma((3,)), dma((3,)), dma(()), dma(()),
        ],
        compiler_params=pltpu.CompilerParams(collective_id=0, has_side_effects=True),
    )(vecs, momenta, perams)


def contract_kernel(
    sources_ref, spins_ref, elem_ref, arrived_ref, out_ref, full, rows, second, wide, tau0, first_op
):
    sn = pl.program_id(0)
    low = lax.broadcasted_iota(jnp.int32, (32, 128), 1) < 64
    even = lax.broadcasted_iota(jnp.int32, (32, 128), 1) % 2 == 0

    def tau(which, quark):
        source, comb = sources_ref[which // 2], which % 2
        spin = spins_ref[comb, quark, 0] * 4 + spins_ref[comb, quark, 1]
        flat = arrived_ref[source, spin].astype(jnp.float32)
        for pair in range(32):
            wide[2 * pair : 2 * pair + 2, :] = flat[:, pair * 128 : (pair + 1) * 128]
        return wide[pl.ds(0, 32, stride=2), :], wide[pl.ds(1, 32, stride=2), :]

    def rolled(value):
        return pltpu.roll(value, 64, 1)

    @pl.when(sn == 0)
    def _():
        full[pl.ds(0, 32, stride=129), :] = jnp.zeros((32, 128), jnp.float32)
        full[pl.ds(96, 32, stride=129), :] = jnp.zeros((32, 128), jnp.float32)
        for q in range(8):
            for group in range(4):
                d = 1 + q + 8 * group
                for odd in range(2):
                    at = group * 64 + odd * 32
                    piece = elem_ref[q, at : at + 32, :].astype(jnp.float32)
                    kodd = (odd + d) % 2
                    e = (odd + d - kodd) // 2
                    base = odd * 64 + kodd * 32 + e
                    full[pl.ds(base, 32 - e, stride=129), :] = piece[: 32 - e]
                    if e:
                        full[pl.ds(129 * (32 - e) + base - 32, e, stride=129), :] = piece[32 - e :]
                    if d < 32:
                        base = 128 * e + kodd * 64 + odd * 32
                        full[pl.ds(base, 32 - e, stride=129), :] = -piece[: 32 - e]
                        if e:
                            full[pl.ds(129 * (32 - e) + base - 4096, e, stride=129), :] = -piece[32 - e :]

        def load_tau0(which, carry):
            real, imag = tau(which, 0)
            upper = jnp.concatenate([real, rolled(real), -imag, -rolled(imag)], axis=0)
            lower = jnp.concatenate([rolled(imag), imag, rolled(real), real], axis=0)
            lanes = lax.broadcasted_iota(jnp.int32, (128, 128), 1)
            tau0[which] = jnp.where(lanes < 64, upper, lower).astype(jnp.bfloat16)
            return carry

        lax.fori_loop(0, 8, load_tau0, 0)
        mine = lax.axis_index("space") % 8
        row = lax.broadcasted_iota(jnp.int32, (16, 128), 0)
        lane = lax.broadcasted_iota(jnp.int32, (16, 128), 1)
        pick = (lane == (row // 8) * 64 + mine * 8 + row % 8).astype(jnp.float32).astype(jnp.bfloat16)
        for which in range(8):
            picked = lax.dot_general(
                pick, tau0[which], (((1,), (1,)), ((), ())), preferred_element_type=jnp.float32
            )
            for part in range(2):
                at = part * 64 + which * 8
                first_op[at : at + 8, :] = picked[part * 8 : part * 8 + 8]
        operator = first_op[...].astype(jnp.bfloat16)
        for p in range(32):
            block = full[p * 128 : (p + 1) * 128, :].astype(jnp.bfloat16)
            first = lax.dot_general(
                operator, block, (((1,), (1,)), ((), ())), preferred_element_type=jnp.float32
            )
            for part in range(2):
                for which in range(8):
                    at = part * 64 + which * 8
                    rows[which, p * 8 : (p + 1) * 8, part * 128 : (part + 1) * 128] = first[at : at + 8]

    real, imag = tau(sn, 2)

    def both_of_pair(value):
        turned, zero = rolled(value), jnp.zeros_like(value)
        return jnp.concatenate(
            [
                jnp.where(low, value, zero),
                jnp.where(low, turned, zero),
                jnp.where(low, zero, turned),
                jnp.where(low, zero, value),
            ],
            axis=0,
        ).astype(jnp.bfloat16)

    kreal, kimag = both_of_pair(real), both_of_pair(imag)
    operand2 = jnp.concatenate(
        [
            jnp.concatenate([kreal, kimag], axis=1),
            jnp.concatenate([-kimag, kreal], axis=1),
        ],
        axis=0,
    )
    product = jnp.dot(rows[sn].astype(jnp.bfloat16), operand2, preferred_element_type=jnp.float32)
    for part in range(2):
        second[part] = product[:, part * 128 : (part + 1) * 128]

    real, imag = tau(sn, 1)

    def arranged(upper, lower):
        uturn, lturn = rolled(upper), rolled(lower)
        straight = jnp.where(low, jnp.where(even, upper, uturn), jnp.where(even, lturn, lower))
        turned = jnp.where(low, jnp.where(even, uturn, upper), jnp.where(even, lower, lturn))
        return [straight, turned]

    operator1 = jnp.concatenate(arranged(real, imag) + arranged(-imag, real), axis=0).astype(jnp.bfloat16)
    row = lax.broadcasted_iota(jnp.int32, (128, 128), 0)
    lane = lax.broadcasted_iota(jnp.int32, (128, 128), 1)
    wanted = (row % 2) * 64 + 2 * (row % 64 // 2) + row // 64
    order = (lane == wanted).astype(jnp.float32).astype(jnp.bfloat16)
    t1 = lax.dot_general(
        order, operator1, (((1,), (1,)), ((), ())), preferred_element_type=jnp.float32
    ).astype(jnp.bfloat16)
    keep = lax.broadcasted_iota(jnp.int32, (64, 128), 1) < 64
    for i in range(8):
        parts = []
        for part in range(2):
            straight = second[part, pl.ds(i, 32, stride=8), :]
            parts += [straight, rolled(straight)]
        operand = jnp.concatenate(parts, axis=0).astype(jnp.bfloat16)
        both = jnp.dot(t1, operand, preferred_element_type=jnp.float32)
        out_ref[i] = jnp.where(keep, both[:64], both[64:])


def contractions(elem, arrived, sources, spins):
    return pl.pallas_call(
        contract_kernel,
        out_shape=jax.ShapeDtypeStruct((64, 64, 128), jnp.float32),
        grid_spec=pltpu.PrefetchScalarGridSpec(
            num_scalar_prefetch=2,
            grid=(8,),
            in_specs=[
                pl.BlockSpec((8, 256, 128), lambda s, *_: (0, 0, 0)),
                pl.BlockSpec((4, 16, 2, 4096), lambda s, *_: (0, 0, 0, 0)),
            ],
            out_specs=pl.BlockSpec((8, 64, 128), lambda s, *_: (s, 0, 0)),
            scratch_shapes=[
                pltpu.VMEM((4096, 128), jnp.float32),
                pltpu.VMEM((8, 256, 256), jnp.float32),
                pltpu.VMEM((2, 256, 128), jnp.float32),
                pltpu.VMEM((64, 128), jnp.float32),
                pltpu.VMEM((8, 128, 128), jnp.bfloat16),
                pltpu.VMEM((128, 128), jnp.float32),
            ],
        ),
        compiler_params=pltpu.CompilerParams(dimension_semantics=("arbitrary",)),
    )(sources, spins, elem, arrived)


def on_device(eigvecs, momenta, perams, sources, spins):
    elem, arrived = elementals(eigvecs[0], momenta, perams[0])
    result = contractions(elem, arrived, sources, spins)
    result = jnp.transpose(result.reshape(64, 32, 2, 128), (0, 2, 1, 3))
    return result.reshape(1, 4, 2, 8, 2, 4096)


def solution(mesh):
    placed = (
        P("tpair", None, None, None, "space"),
        P(),
        P("tpair", None, None, None, None),
        P(),
        P(),
    )
    return jax.shard_map(
        on_device,
        mesh=mesh,
        in_specs=placed,
        out_specs=P("tpair", None, None, "space", None, None),
        check_vma=False,
    )
```

```python
import jax
import jax.numpy as jnp
from jax import lax
from jax.experimental import pallas as pl
from jax.experimental.pallas import tpu as pltpu
from jax.sharding import PartitionSpec as P

LEXT = 64
TWO_PI = 6.283185307179586
MESH = pl.DeviceIdType.MESH

NX, NZ, NC = 4, 8, 2
NY = 4
HALF = NZ // 2


def place():
    index = lax.axis_index("space")
    return index // (NZ * NC), (index // NC) % NZ, index % NC


def at_space(x, z, c):
    return {"space": (x * NZ + z) * NC + c}


def elemental_kernel(
    vec_ref, mom_ref, sources_ref, spins_ref, per_ref, rows_ref, second_op_ref, third_op_ref,
    cosines, sines, fields, vfloat, left, right, total, outbox, inbox, chunk, all_chunks,
    arrived, wide, full, first_op, ring_send, ring_recv, pair_send, pair_recv, sum_send, sum_recv,
    share_send, share_recv, swap_send, swap_recv, per_send, per_recv, per_own, own_sem,
):
    x, z, c = place()
    y = lax.axis_index("tpair")
    zhalf, zz = z // HALF, z % HALF
    slot_q = zz * NC + c
    on_right = at_space(x, (z + 1) % NZ, c)
    on_left = at_space(x, (z + NZ - 1) % NZ, c)
    partner = at_space(x, z, 1 - c)
    across = [at_space((x + step) % NX, z, c) for step in range(1, NX)]
    along = [at_space(x, zhalf * HALF + (zz + step) % HALF, c) for step in range(1, HALF)]
    sinks = [{"tpair": (y + step) % NY} for step in range(1, NY)]

    barrier = pltpu.get_barrier_semaphore()
    greeted = [on_right, on_left, partner] + across + along + sinks
    for target in greeted:
        pl.semaphore_signal(barrier, inc=1, device_id=target, device_id_type=MESH)
    own = pltpu.make_async_copy(vec_ref, fields.at[0, 0], own_sem)
    own.start()
    pl.semaphore_wait(barrier, len(greeted))
    own.wait()

    def ring_copy(rel, colour, rightward):
        there = (rel + NZ - 1) % NZ if rightward else (rel + 1) % NZ
        return pltpu.make_async_remote_copy(
            src_ref=fields.at[0, rel, :, colour],
            dst_ref=fields.at[0, there, :, colour],
            send_sem=ring_send.at[there, colour],
            recv_sem=ring_recv.at[there, colour],
            device_id=on_right if rightward else on_left,
            device_id_type=MESH,
        )

    def ring_arrival(rel, colour):
        return pltpu.make_async_remote_copy(
            src_ref=fields.at[0, rel, :, colour],
            dst_ref=fields.at[0, rel, :, colour],
            send_sem=ring_send.at[rel, colour],
            recv_sem=ring_recv.at[rel, colour],
            device_id=on_right,
            device_id_type=MESH,
        )

    def pair_copy(rel, colour):
        return pltpu.make_async_remote_copy(
            src_ref=fields.at[0, rel, :, colour],
            dst_ref=fields.at[1, rel, :, colour],
            send_sem=pair_send.at[rel, colour],
            recv_sem=pair_recv.at[rel, colour],
            device_id=partner,
            device_id_type=MESH,
        )

    for colour in range(3):
        ring_copy(0, colour, True).start()
        ring_copy(0, colour, False).start()
        pair_copy(0, colour).start()

    per_copies = []
    for step in range(1, NY):
        other = (y + step) % NY
        copy = pltpu.make_async_remote_copy(
            src_ref=per_ref.at[other],
            dst_ref=arrived.at[y],
            send_sem=per_send.at[step - 1],
            recv_sem=per_recv.at[step - 1],
            device_id=sinks[step - 1],
            device_id_type=MESH,
        )
        copy.start()
        per_copies.append(copy)
    per_local = pltpu.make_async_copy(per_ref.at[y], arrived.at[y], per_own)
    per_local.start()

    def relay(place_in_order):
        rel = jnp.where(place_in_order % 2 == 1, NZ - (place_in_order + 1) // 2, place_in_order // 2)
        for colour in range(3):
            ring_arrival(rel, colour).wait_recv()

            @pl.when((place_in_order % 2 == 1) & (place_in_order < 7))
            def _():
                ring_copy(rel, colour, True).start()

            @pl.when((place_in_order % 2 == 0) & (place_in_order < 6))
            def _():
                ring_copy(rel, colour, False).start()

            pair_copy(rel, colour).start()

    row = lax.broadcasted_iota(jnp.int32, (NC * NZ, 128), 0)
    lane = lax.broadcasted_iota(jnp.int32, (NC * NZ, 128), 1)
    core = jnp.where(row < NZ, c, 1 - c)
    sites = ((x * NZ + ((z + row) & (NZ - 1))) * NC + core) * 128 + lane
    xs, ys, zs = sites & (LEXT - 1), (sites >> 6) & (LEXT - 1), sites >> 12
    factor = lax.rsqrt(jnp.float32(24.0 * 128 * NX * NZ * NC))
    for mom in range(4):
        mine = 2 * mom + zhalf
        turns = mom_ref[0, mine] * xs + mom_ref[1, mine] * ys + mom_ref[2, mine] * zs
        angle = (turns & (LEXT - 1)).astype(jnp.float32) * (TWO_PI / LEXT)
        cosines[mom] = jnp.cos(angle) * factor
        sines[mom] = jnp.sin(angle) * factor

    total[...] = jnp.zeros_like(total)

    def contract(core_slot, rel):
        for part in range(2):
            for colour in range(3):
                values = fields[core_slot, rel, part, colour].astype(jnp.float32)
                vfloat[part, colour, 0:64] = values
                vfloat[part, colour, 64:128] = values
        for colour in range(3):
            nxt, aft = (colour + 1) % 3, (colour + 2) % 3
            for odd in range(2):
                rows = pl.ds(odd, 32, stride=2)
                lrn, lin = vfloat[0, nxt, rows], vfloat[1, nxt, rows]
                lra, lia = vfloat[0, aft, rows], vfloat[1, aft, rows]
                for group in range(4):
                    rows = pl.ds(1 + slot_q + 8 * group + odd, 32, stride=2)
                    rrn, rin = vfloat[0, nxt, rows], vfloat[1, nxt, rows]
                    rra, ria = vfloat[0, aft, rows], vfloat[1, aft, rows]
                    real = lrn * rra - lin * ria - (lra * rrn - lia * rin)
                    imag = lrn * ria + lin * rra - (lra * rin + lia * rrn)
                    where = pl.ds(group * 64 + odd * 32, 32)
                    left[where, colour * 128 : (colour + 1) * 128] = real.astype(jnp.bfloat16)
                    left[where, (3 + colour) * 128 : (4 + colour) * 128] = imag.astype(jnp.bfloat16)
        at = pl.ds(core_slot * NZ + rel, 1)
        for colour in range(3):
            for odd in range(2):
                rows = pl.ds(odd, 32, stride=2)
                vr, vi = vfloat[0, colour, rows], vfloat[1, colour, rows]
                for mom in range(4):
                    cosine, sine = cosines[mom, at, :], sines[mom, at, :]
                    pr = (cosine * vr + sine * vi).astype(jnp.bfloat16)
                    pi = (cosine * vi - sine * vr).astype(jnp.bfloat16)
                    upper, lower = pl.ds(mom * 128 + odd * 32, 32), pl.ds(mom * 128 + 64 + odd * 32, 32)
                    first, second = pl.ds(colour * 128, 128), pl.ds((3 + colour) * 128, 128)
                    right[upper, first] = pr
                    right[upper, second] = -pi
                    right[lower, first] = pi
                    right[lower, second] = pr
        product = lax.dot_general(
            left[...], right[...], (((1,), (1,)), ((), ())), preferred_element_type=jnp.float32
        )
        for mom in range(4):
            total[mom] += product[:, mom * 128 : (mom + 1) * 128]

    def body(n, carry):
        rel = jnp.where(n % 2 == 1, NZ - (n + 1) // 2, n // 2)
        contract(0, rel)

        @pl.when(n == 0)
        def _():
            relay(1)

        @pl.when(n < 6)
        def _():
            relay(n + 2)

        for colour in range(3):
            pair_copy(rel, colour).wait_recv()
        contract(1, rel)
        return carry

    lax.fori_loop(0, NZ, body, 0)

    def sum_copy(group, step):
        return pltpu.make_async_remote_copy(
            src_ref=outbox.at[step - 1, group],
            dst_ref=inbox.at[step - 1, group],
            send_sem=sum_send.at[group, step - 1],
            recv_sem=sum_recv.at[group, step - 1],
            device_id=across[step - 1],
            device_id_type=MESH,
        )

    def share_copy(group, step):
        return pltpu.make_async_remote_copy(
            src_ref=chunk.at[group],
            dst_ref=all_chunks.at[group, slot_q],
            send_sem=share_send.at[group, step - 1],
            recv_sem=share_recv.at[group, step - 1],
            device_id=along[step - 1],
            device_id_type=MESH,
        )

    def share_arrival(group, step):
        return pltpu.make_async_remote_copy(
            src_ref=chunk.at[group],
            dst_ref=all_chunks.at[group, (zz + HALF - step) % HALF * NC + c],
            send_sem=share_send.at[group, step - 1],
            recv_sem=share_recv.at[group, step - 1],
            device_id=along[step - 1],
            device_id_type=MESH,
        )

    def swap_copy(group, step, core):
        slot = (zz + HALF - step) % HALF * NC + core
        return pltpu.make_async_remote_copy(
            src_ref=chunk.at[group] if step == 0 else all_chunks.at[group, slot],
            dst_ref=all_chunks.at[group, slot],
            send_sem=swap_send.at[group, step],
            recv_sem=swap_recv.at[group, step],
            device_id=partner,
            device_id_type=MESH,
        )

    for group in range(4):
        where = pl.ds(group * 64, 64)
        for step in (2, 1, 3):
            outbox[step - 1, group] = total[(x + step) % NX, where].astype(jnp.bfloat16)
            sum_copy(group, step).start()

    per_local.wait()
    for step, copy in enumerate(per_copies, 1):
        copy.wait_send()
        pltpu.make_async_remote_copy(
            src_ref=per_ref.at[y],
            dst_ref=arrived.at[(y + NY - step) % NY],
            send_sem=per_send.at[step - 1],
            recv_sem=per_recv.at[step - 1],
            device_id=sinks[step - 1],
            device_id_type=MESH,
        ).wait_recv()

    low = lax.broadcasted_iota(jnp.int32, (32, 128), 1) < 64
    even = lax.broadcasted_iota(jnp.int32, (32, 128), 1) % 2 == 0
    row = lax.broadcasted_iota(jnp.int32, (16, 128), 0)
    lane = lax.broadcasted_iota(jnp.int32, (16, 128), 1)
    rank = lax.axis_index("space") % 8
    pick = (lane == (row // 8) * 64 + rank * 8 + row % 8).astype(jnp.float32).astype(jnp.bfloat16)
    row = lax.broadcasted_iota(jnp.int32, (128, 128), 0)
    lane = lax.broadcasted_iota(jnp.int32, (128, 128), 1)
    wanted = (row % 2) * 64 + 2 * (row % 64 // 2) + row // 64
    order = (lane == wanted).astype(jnp.float32).astype(jnp.bfloat16)

    def rolled(value):
        return pltpu.roll(value, 64, 1)

    def tau(which, quark):
        source, comb = sources_ref[which // 2], which % 2
        spin = spins_ref[comb, 0, quark] * 4 + spins_ref[comb, 1, quark]
        flat = arrived[source, spin].astype(jnp.float32)
        for pair in range(32):
            wide[quark, 2 * pair : 2 * pair + 2, :] = flat[:, pair * 128 : (pair + 1) * 128]
        return wide[quark, pl.ds(0, 32, stride=2), :], wide[quark, pl.ds(1, 32, stride=2), :]

    def both_of_pair(value):
        turned, zero = rolled(value), jnp.zeros_like(value)
        return jnp.concatenate(
            [
                jnp.where(low, value, zero),
                jnp.where(low, turned, zero),
                jnp.where(low, zero, turned),
                jnp.where(low, zero, value),
            ],
            axis=0,
        ).astype(jnp.bfloat16)

    def arranged(upper, lower):
        uturn, lturn = rolled(upper), rolled(lower)
        straight = jnp.where(low, jnp.where(even, upper, uturn), jnp.where(even, lturn, lower))
        turned = jnp.where(low, jnp.where(even, uturn, upper), jnp.where(even, lower, lturn))
        return [straight, turned]

    def operators(which, carry):
        real, imag = tau(which, 0)
        upper = jnp.concatenate([real, rolled(real), -imag, -rolled(imag)], axis=0)
        lower = jnp.concatenate([rolled(imag), imag, rolled(real), real], axis=0)
        lanes = lax.broadcasted_iota(jnp.int32, (128, 128), 1)
        picked = lax.dot_general(
            pick,
            jnp.where(lanes < 64, upper, lower).astype(jnp.bfloat16),
            (((1,), (1,)), ((), ())),
            preferred_element_type=jnp.float32,
        )
        for part in range(2):
            at = pl.ds(pl.multiple_of(part * 64 + which * 8, 8), 8)
            first_op[at, :] = picked[part * 8 : part * 8 + 8]
        real, imag = tau(which, 2)
        second_op_ref[which, 0] = both_of_pair(real)
        second_op_ref[which, 1] = both_of_pair(imag)
        real, imag = tau(which, 1)
        operator = jnp.concatenate(arranged(real, imag) + arranged(-imag, real), axis=0)
        third_op_ref[which] = lax.dot_general(
            order, operator.astype(jnp.bfloat16), (((1,), (1,)), ((), ())),
            preferred_element_type=jnp.float32,
        ).astype(jnp.bfloat16)
        return carry

    lax.fori_loop(0, 4, operators, 0)

    for group in range(4):
        where = pl.ds(group * 64, 64)
        for step in (1, 2, 3):
            sum_copy(group, step).wait_recv()
        summed = total[x, where]
        for step in range(3):
            summed = summed + inbox[step, group].astype(jnp.float32)
        chunk[group] = summed.astype(jnp.bfloat16)
        for step in (3, 2, 1):
            share_copy(group, step).start()
        swap_copy(group, 0, c).start()
        all_chunks[group, slot_q] = chunk[group]

    lax.fori_loop(4, 8, operators, 0)
    full[pl.ds(0, 32, stride=129), :] = jnp.zeros((32, 128), jnp.float32)
    full[pl.ds(96, 32, stride=129), :] = jnp.zeros((32, 128), jnp.float32)

    def onward(group):
        for step in (1, 3, 2):
            share_arrival(group, step).wait_recv()
            swap_copy(group, step, c).start()

    def expand(group):
        for step in range(HALF):
            swap_copy(group, step, 1 - c).wait_recv()
        for q in range(8):
            d = 1 + q + 8 * group
            for odd in range(2):
                piece = all_chunks[group, q, odd * 32 : odd * 32 + 32, :].astype(jnp.float32)
                kodd = (odd + d) % 2
                e = (odd + d - kodd) // 2
                base = odd * 64 + kodd * 32 + e
                full[pl.ds(base, 32 - e, stride=129), :] = piece[: 32 - e]
                if e:
                    full[pl.ds(129 * (32 - e) + base - 32, e, stride=129), :] = piece[32 - e :]
                if d < 32:
                    base = 128 * e + kodd * 64 + odd * 32
                    full[pl.ds(base, 32 - e, stride=129), :] = -piece[: 32 - e]
                    if e:
                        full[pl.ds(129 * (32 - e) + base - 4096, e, stride=129), :] = -piece[32 - e :]

    onward(0)
    onward(1)
    expand(0)
    onward(2)
    expand(1)
    onward(3)
    expand(2)
    expand(3)

    operator = first_op[...].astype(jnp.bfloat16)
    for two in range(16):
        block = full[two * 256 : (two + 1) * 256, :].astype(jnp.bfloat16)
        first = lax.dot_general(
            operator, block, (((1,), (1,)), ((), ())), preferred_element_type=jnp.float32
        )
        for part in range(2):
            for which in range(8):
                at = part * 64 + which * 8
                piece = jnp.concatenate([first[at : at + 8, :128], first[at : at + 8, 128:]], axis=0)
                rows_ref[which, two * 16 : two * 16 + 16, part * 128 : (part + 1) * 128] = piece.astype(jnp.bfloat16)

    for rel in range(NZ):
        for colour in range(3):
            if rel in (7, 6, 5, 4):
                ring_copy((rel + 1) % NZ, colour, True).wait_send()
            elif rel:
                ring_copy(rel - 1, colour, False).wait_send()
            pair_copy(rel, colour).wait_send()
    for group in range(4):
        for step in (1, 2, 3):
            sum_copy(group, step).wait_send()
            share_copy(group, step).wait_send()
        for step in range(HALF):
            swap_copy(group, step, c).wait_send()


def first_contraction(vecs, momenta, sources, spins, perams):
    vmem = pl.BlockSpec(memory_space=pltpu.VMEM)
    smem = pl.BlockSpec(memory_space=pltpu.SMEM)
    dma, bf16, f32 = pltpu.SemaphoreType.DMA, jnp.bfloat16, jnp.float32
    return pl.pallas_call(
        elemental_kernel,
        out_shape=(
            jax.ShapeDtypeStruct((8, 256, 256), bf16),
            jax.ShapeDtypeStruct((8, 2, 128, 128), bf16),
            jax.ShapeDtypeStruct((8, 128, 128), bf16),
        ),
        in_specs=[vmem, smem, smem, smem, pl.BlockSpec(memory_space=pl.ANY)],
        out_specs=(vmem, vmem, vmem),
        scratch_shapes=[
            pltpu.VMEM((4, NC * NZ, 128), f32),
            pltpu.VMEM((4, NC * NZ, 128), f32),
            pltpu.VMEM((NC, NZ, 2, 3, 64, 128), bf16),
            pltpu.VMEM((2, 3, 128, 128), f32),
            pltpu.VMEM((256, 768), bf16),
            pltpu.VMEM((512, 768), bf16),
            pltpu.VMEM((4, 256, 128), f32),
            pltpu.VMEM((3, 4, 64, 128), bf16),
            pltpu.VMEM((3, 4, 64, 128), bf16),
            pltpu.VMEM((4, 64, 128), bf16),
            pltpu.VMEM((4, 8, 64, 128), bf16),
            pltpu.VMEM(perams.shape, bf16),
            pltpu.VMEM((3, 64, 128), f32),
            pltpu.VMEM((4096, 128), f32),
            pltpu.VMEM((128, 128), f32),
            dma((NZ, 3)), dma((NZ, 3)), dma((NZ, 3)), dma((NZ, 3)),
            dma((4, 3)), dma((4, 3)), dma((4, 3)), dma((4, 3)), dma((4, 4)), dma((4, 4)),
            dma((3,)), dma((3,)), dma(()), dma(()),
        ],
        compiler_params=pltpu.CompilerParams(collective_id=0, has_side_effects=True),
    )(vecs, momenta, sources, spins, perams)


def contract_kernel(rows_ref, second_op_ref, third_op_ref, out_ref, second):
    kreal, kimag = second_op_ref[0, 0], second_op_ref[0, 1]
    operator = jnp.concatenate(
        [jnp.concatenate([kreal, kimag], axis=1), jnp.concatenate([-kimag, kreal], axis=1)], axis=0
    )
    product = jnp.dot(rows_ref[0], operator, preferred_element_type=jnp.float32)
    for part in range(2):
        second[part] = product[:, part * 128 : (part + 1) * 128]
    keep = lax.broadcasted_iota(jnp.int32, (64, 128), 1) < 64
    for i in range(8):
        parts = []
        for part in range(2):
            straight = second[part, pl.ds(i, 32, stride=8), :]
            parts += [straight, pltpu.roll(straight, 64, 1)]
        operand = jnp.concatenate(parts, axis=0).astype(jnp.bfloat16)
        both = jnp.dot(third_op_ref[0], operand, preferred_element_type=jnp.float32)
        out_ref[i] = jnp.where(keep, both[:64], both[64:])


def last_contractions(rows, second_op, third_op):
    return pl.pallas_call(
        contract_kernel,
        grid=(8,),
        out_shape=jax.ShapeDtypeStruct((64, 64, 128), jnp.float32),
        in_specs=[
            pl.BlockSpec((1, 256, 256), lambda s: (s, 0, 0)),
            pl.BlockSpec((1, 2, 128, 128), lambda s: (s, 0, 0, 0)),
            pl.BlockSpec((1, 128, 128), lambda s: (s, 0, 0)),
        ],
        out_specs=pl.BlockSpec((8, 64, 128), lambda s: (s, 0, 0)),
        scratch_shapes=[pltpu.VMEM((2, 256, 128), jnp.float32)],
        compiler_params=pltpu.CompilerParams(dimension_semantics=("arbitrary",)),
    )(rows, second_op, third_op)


def on_device(eigvecs, momenta, perams, sources, spins):
    operands = first_contraction(
        eigvecs[0], jnp.transpose(momenta), sources, jnp.transpose(spins, (0, 2, 1)), perams[0]
    )
    result = last_contractions(*operands)
    result = jnp.transpose(result.reshape(64, 32, 2, 128), (0, 2, 1, 3))
    return result.reshape(1, 4, 2, 8, 2, 4096)


def solution(mesh):
    placed = (
        P("tpair", None, None, None, "space"),
        P(),
        P("tpair", None, None, None, None),
        P(),
        P(),
    )
    return jax.shard_map(
        on_device,
        mesh=mesh,
        in_specs=placed,
        out_specs=P("tpair", None, None, "space", None, None),
        check_vma=False,
    )
```

```python
import functools

import jax
import jax.numpy as jnp
from jax import lax
from jax.experimental import pallas as pl
from jax.experimental.pallas import tpu as pltpu
from jax.sharding import PartitionSpec as P

LEXT = 64
TWO_PI = 6.283185307179586
MESH = pl.DeviceIdType.MESH

NX, NZ, NC = 4, 8, 2
NY = 4
HALF = NZ // 2
PER_STEP = 2


def place():
    index = lax.axis_index("space")
    return lax.div(index, NZ * NC), lax.rem(lax.div(index, NC), NZ), lax.rem(index, NC)


def at_space(x, z, c):
    return {"space": (x * NZ + z) * NC + c}


def elemental_kernel(
    vec_ref, mom_hbm, sources_hbm, spins_hbm, per_ref, rows_ref, second_op_ref, third_op_ref,
    cosines, sines, fields, vfloat, left, right, total, core_in, own_sum, outbox, inbox, chunk, all_chunks,
    arrived, wide, full, first_op, mom_ref, sources_ref, spins_ref, small_sem, own_sem, ring_send, ring_recv, core_send, core_recv, sum_send, sum_recv,
    share_send, share_recv, swap_send, swap_recv, per_send, per_recv, per_own,
):
    x, z, c = place()
    y = lax.axis_index("tpair")
    zhalf, zz = lax.div(z, HALF), lax.rem(z, HALF)
    slot_q = zz * NC + c
    on_right = at_space(x, lax.rem(z + 1, NZ), c)
    on_left = at_space(x, lax.rem(z + NZ - 1, NZ), c)
    partner = at_space(x, z, 1 - c)
    across = [at_space(lax.rem(x + step, NX), z, c) for step in range(1, NX)]
    along = [at_space(x, zhalf * HALF + lax.rem(zz + step, HALF), c) for step in range(1, HALF)]
    sinks = [{"tpair": lax.rem(y + step, NY)} for step in range(1, NY)]

    barrier = pltpu.get_barrier_semaphore()
    greeted = [on_right, on_left, partner] + across + along + sinks
    for target in greeted:
        pl.semaphore_signal(barrier, inc=1, device_id=target, device_id_type=MESH)
    own = pltpu.make_async_copy(vec_ref, fields.at[0], own_sem)
    own.start()
    small = [
        pltpu.make_async_copy(mom_hbm, mom_ref, small_sem.at[0]),
        pltpu.make_async_copy(sources_hbm, sources_ref, small_sem.at[1]),
        pltpu.make_async_copy(spins_hbm, spins_ref, small_sem.at[2]),
    ]
    for copy in small:
        copy.start()
    pl.semaphore_wait(barrier, len(greeted))
    own.wait()

    def remote(source, target, send_sem, recv_sem, device):
        return pltpu.make_async_remote_copy(
            src_ref=source, dst_ref=target, send_sem=send_sem, recv_sem=recv_sem,
            device_id=device, device_id_type=MESH,
        )

    def ring_copy(rel, part, rightward):
        there = (rel + NZ - 1) % NZ if rightward else (rel + 1) % NZ
        return remote(
            fields.at[rel, part], fields.at[there, part], ring_send, ring_recv.at[there, part],
            on_right if rightward else on_left,
        )

    for part in range(2):
        ring_copy(0, part, True).start()
        ring_copy(0, part, False).start()

    for step in range(1, NY):
        remote(per_ref.at[lax.rem(y + step, NY)], arrived.at[y], per_send, per_recv, sinks[step - 1]).start()
    per_local = pltpu.make_async_copy(per_ref.at[y], arrived.at[y], per_own)
    per_local.start()

    def relay(step):
        for part in range(2):
            if step < HALF or part == 0:
                rel = NZ - step
                remote(fields.at[rel, part], fields.at[rel, part], ring_send, ring_recv.at[rel, part], on_right).wait_recv()
                if step < HALF - 1 or (step == HALF - 1 and part == 0):
                    ring_copy(rel, part, True).start()
            if step < HALF or part == 1:
                rel = step
                remote(fields.at[rel, part], fields.at[rel, part], ring_send, ring_recv.at[rel, part], on_left).wait_recv()
                if step < HALF - 1 or (step == HALF - 1 and part == 1):
                    ring_copy(rel, part, False).start()

    for copy in small:
        copy.wait()

    row = lax.broadcasted_iota(jnp.int32, (NZ, 128), 0)
    lane = lax.broadcasted_iota(jnp.int32, (NZ, 128), 1)
    sites = ((x * NZ + ((z + row) & (NZ - 1))) * NC + c) * 128 + lane
    xs, ys, zs = sites & (LEXT - 1), (sites >> 6) & (LEXT - 1), sites >> 12
    factor = lax.rsqrt(jnp.float32(24.0 * 128 * NX * NZ * NC))
    for mom in range(4):
        mine = 2 * mom + zhalf
        turns = mom_ref[0, mine] * xs + mom_ref[1, mine] * ys + mom_ref[2, mine] * zs
        angle = (turns & (LEXT - 1)).astype(jnp.float32) * (TWO_PI / LEXT)
        cosines[mom] = jnp.cos(angle) * factor
        sines[mom] = jnp.sin(angle) * factor

    total[...] = jnp.zeros_like(total)

    def contract(rel):
        for part in range(2):
            for colour in range(3):
                values = fields[rel, part, colour].astype(jnp.float32)
                vfloat[part, colour, 0:64] = values
                vfloat[part, colour, 64:128] = values
        for colour in range(3):
            nxt, aft = (colour + 1) % 3, (colour + 2) % 3
            for odd in range(2):
                rows = pl.ds(odd, 32, stride=2)
                lrn, lin = vfloat[0, nxt, rows], vfloat[1, nxt, rows]
                lra, lia = vfloat[0, aft, rows], vfloat[1, aft, rows]
                for core in range(2):
                    for group in range(4):
                        rows = pl.ds(1 + zz * NC + core + 8 * group + odd, 32, stride=2)
                        rrn, rin = vfloat[0, nxt, rows], vfloat[1, nxt, rows]
                        rra, ria = vfloat[0, aft, rows], vfloat[1, aft, rows]
                        real = lrn * rra - lin * ria - (lra * rrn - lia * rin)
                        imag = lrn * ria + lin * rra - (lra * rin + lia * rrn)
                        where = pl.ds(core * 256 + group * 64 + odd * 32, 32)
                        left[where, colour * 128 : (colour + 1) * 128] = real.astype(jnp.bfloat16)
                        left[where, (3 + colour) * 128 : (4 + colour) * 128] = imag.astype(jnp.bfloat16)
        at = pl.ds(rel, 1)
        for colour in range(3):
            for odd in range(2):
                rows = pl.ds(odd, 32, stride=2)
                vr, vi = vfloat[0, colour, rows], vfloat[1, colour, rows]
                for mom in range(4):
                    cosine, sine = cosines[mom, at, :], sines[mom, at, :]
                    pr = (cosine * vr + sine * vi).astype(jnp.bfloat16)
                    pi = (cosine * vi - sine * vr).astype(jnp.bfloat16)
                    upper, lower = pl.ds(mom * 128 + odd * 32, 32), pl.ds(mom * 128 + 64 + odd * 32, 32)
                    first, second = pl.ds(colour * 128, 128), pl.ds((3 + colour) * 128, 128)
                    right[upper, first] = pr
                    right[upper, second] = -pi
                    right[lower, first] = pi
                    right[lower, second] = pr
        product = lax.dot_general(
            left[...], right[...], (((1,), (1,)), ((), ())), preferred_element_type=jnp.float32
        )
        for core in range(2):
            for group in range(4):
                at = core * 256 + group * 64
                for mom in range(4):
                    total[core, group, mom] += product[at : at + 64, mom * 128 : (mom + 1) * 128]

    def body(n, carry):
        contract(jnp.where(n % 2 == 1, NZ - (n + 1) // 2, n // 2))
        for after, step in ((0, 1), (1, 2), (3, 3), (5, 4)):
            pl.when(n == after)(functools.partial(relay, step))
        return carry

    lax.fori_loop(0, NZ, body, 0)

    for group in range(4):
        remote(total.at[1 - c, group], core_in.at[group], core_send, core_recv.at[group], partner).start()

    def share_arrival(group, step):
        owner = lax.rem(zz + HALF - step, HALF) * NC + c
        return remote(
            chunk.at[group], all_chunks.at[group, owner], share_send, share_recv.at[group, step - 1], along[step - 1]
        )

    def swap_copy(group, step):
        owner = lax.rem(zz + HALF - step, HALF) * NC + c
        return remote(
            chunk.at[group] if step == 0 else all_chunks.at[group, owner],
            all_chunks.at[group, owner], swap_send, swap_recv.at[group], partner,
        )

    per_local.wait()
    remote(per_ref.at[0:3], arrived.at[0:3], per_send, per_recv, sinks[0]).wait()

    low = lax.broadcasted_iota(jnp.int32, (32, 128), 1) < 64
    even = lax.broadcasted_iota(jnp.int32, (32, 128), 1) % 2 == 0
    row = lax.broadcasted_iota(jnp.int32, (16, 128), 0)
    lane = lax.broadcasted_iota(jnp.int32, (16, 128), 1)
    rank = lax.axis_index("space") % 8
    pick = (lane == (row // 8) * 64 + rank * 8 + row % 8).astype(jnp.float32).astype(jnp.bfloat16)
    row = lax.broadcasted_iota(jnp.int32, (128, 128), 0)
    lane = lax.broadcasted_iota(jnp.int32, (128, 128), 1)
    wanted = (row % 2) * 64 + 2 * (row % 64 // 2) + row // 64
    order = (lane == wanted).astype(jnp.float32).astype(jnp.bfloat16)

    def rolled(value):
        return pltpu.roll(value, 64, 1)

    def tau(which, quark):
        source, comb = sources_ref[which // 2], which % 2
        spin = spins_ref[comb, 0, quark] * 4 + spins_ref[comb, 1, quark]
        flat = arrived[source, spin].astype(jnp.float32)
        for pair in range(32):
            wide[quark, 2 * pair : 2 * pair + 2, :] = flat[:, pair * 128 : (pair + 1) * 128]
        return wide[quark, pl.ds(0, 32, stride=2), :], wide[quark, pl.ds(1, 32, stride=2), :]

    def both_of_pair(value):
        turned, zero = rolled(value), jnp.zeros_like(value)
        return jnp.concatenate(
            [
                jnp.where(low, value, zero),
                jnp.where(low, turned, zero),
                jnp.where(low, zero, turned),
                jnp.where(low, zero, value),
            ],
            axis=0,
        ).astype(jnp.bfloat16)

    def arranged(upper, lower):
        uturn, lturn = rolled(upper), rolled(lower)
        straight = jnp.where(low, jnp.where(even, upper, uturn), jnp.where(even, lturn, lower))
        turned = jnp.where(low, jnp.where(even, uturn, upper), jnp.where(even, lower, lturn))
        return [straight, turned]

    def operators(which, carry):
        real, imag = tau(which, 0)
        upper = jnp.concatenate([real, rolled(real), -imag, -rolled(imag)], axis=0)
        lower = jnp.concatenate([rolled(imag), imag, rolled(real), real], axis=0)
        lanes = lax.broadcasted_iota(jnp.int32, (128, 128), 1)
        picked = lax.dot_general(
            pick,
            jnp.where(lanes < 64, upper, lower).astype(jnp.bfloat16),
            (((1,), (1,)), ((), ())),
            preferred_element_type=jnp.float32,
        )
        for part in range(2):
            at = pl.ds(pl.multiple_of(part * 64 + which * 8, 8), 8)
            first_op[at, :] = picked[part * 8 : part * 8 + 8]
        real, imag = tau(which, 2)
        second_op_ref[which, 0] = both_of_pair(real)
        second_op_ref[which, 1] = both_of_pair(imag)
        real, imag = tau(which, 1)
        operator = jnp.concatenate(arranged(real, imag) + arranged(-imag, real), axis=0)
        third_op_ref[which] = lax.dot_general(
            order, operator.astype(jnp.bfloat16), (((1,), (1,)), ((), ())),
            preferred_element_type=jnp.float32,
        ).astype(jnp.bfloat16)
        return carry

    lax.fori_loop(0, 2, operators, 0)

    for group in range(4):
        remote(core_in.at[group], core_in.at[group], core_send, core_recv.at[group], partner).wait_recv()
        for step in (2, 1, 3):
            mom = lax.rem(x + step, NX)
            outbox[group, step - 1] = (total[c, group, mom] + core_in[group, mom]).astype(jnp.bfloat16)
            remote(
                outbox.at[group, step - 1], inbox.at[group, step - 1], sum_send, sum_recv.at[group], across[step - 1]
            ).start()
        own_sum[group] = total[c, group, x] + core_in[group, x]

    lax.fori_loop(2, 5, operators, 0)

    for group in range(4):
        remote(inbox.at[group], inbox.at[group], sum_send, sum_recv.at[group], across[0]).wait_recv()
        summed = own_sum[group]
        for step in range(3):
            summed = summed + inbox[group, step].astype(jnp.float32)
        chunk[group] = summed.astype(jnp.bfloat16)
        for step in (3, 2, 1):
            remote(
                chunk.at[group], all_chunks.at[group, slot_q], share_send, share_recv.at[group, step - 1], along[step - 1]
            ).start()
        swap_copy(group, 0).start()
        all_chunks[group, slot_q] = chunk[group]

    lax.fori_loop(5, 8, operators, 0)
    full[pl.ds(0, 32, stride=129), :] = jnp.zeros((32, 128), jnp.float32)
    full[pl.ds(96, 32, stride=129), :] = jnp.zeros((32, 128), jnp.float32)

    def onward(group):
        for step in (1, 3, 2):
            share_arrival(group, step).wait_recv()
            swap_copy(group, step).start()

    def expand(group):
        remote(chunk, chunk, swap_send, swap_recv.at[group], partner).wait_recv()
        for q in range(8):
            d = 1 + q + 8 * group
            for odd in range(2):
                piece = all_chunks[group, q, odd * 32 : odd * 32 + 32, :].astype(jnp.float32)
                kodd = (odd + d) % 2
                e = (odd + d - kodd) // 2
                base = odd * 64 + kodd * 32 + e
                full[pl.ds(base, 32 - e, stride=129), :] = piece[: 32 - e]
                if e:
                    full[pl.ds(129 * (32 - e) + base - 32, e, stride=129), :] = piece[32 - e :]
                if d < 32:
                    base = 128 * e + kodd * 64 + odd * 32
                    full[pl.ds(base, 32 - e, stride=129), :] = -piece[: 32 - e]
                    if e:
                        full[pl.ds(129 * (32 - e) + base - 4096, e, stride=129), :] = -piece[32 - e :]

    onward(0)
    onward(1)
    expand(0)
    onward(2)
    expand(1)
    onward(3)
    expand(2)
    expand(3)

    operator = first_op[...].astype(jnp.bfloat16)
    for two in range(16):
        block = full[two * 256 : (two + 1) * 256, :].astype(jnp.bfloat16)
        first = lax.dot_general(
            operator, block, (((1,), (1,)), ((), ())), preferred_element_type=jnp.float32
        )
        for part in range(2):
            for which in range(8):
                at = part * 64 + which * 8
                piece = jnp.concatenate([first[at : at + 8, :128], first[at : at + 8, 128:]], axis=0)
                rows_ref[which, two * 16 : two * 16 + 16, part * 128 : (part + 1) * 128] = piece.astype(jnp.bfloat16)

    remote(fields.at[0:7], fields.at[0:7], ring_send, ring_recv.at[0, 0], on_right).wait_send()
    remote(core_in, core_in, core_send, core_recv.at[0], partner).wait_send()
    remote(outbox, inbox, sum_send, sum_recv.at[0], across[0]).wait_send()
    remote(outbox, inbox, share_send, share_recv.at[0, 0], along[0]).wait_send()
    remote(all_chunks.at[0:2], all_chunks.at[0:2], swap_send, swap_recv.at[0], partner).wait_send()


def first_contraction(vecs, momenta, sources, spins, perams):
    vmem = pl.BlockSpec(memory_space=pltpu.VMEM)
    hbm = pl.BlockSpec(memory_space=pltpu.HBM)
    dma, bf16, f32 = pltpu.SemaphoreType.DMA, jnp.bfloat16, jnp.float32
    return pl.pallas_call(
        elemental_kernel,
        out_shape=(
            jax.ShapeDtypeStruct((8, 256, 256), bf16),
            jax.ShapeDtypeStruct((8, 2, 128, 128), bf16),
            jax.ShapeDtypeStruct((8, 128, 128), bf16),
        ),
        in_specs=[hbm, hbm, hbm, hbm, hbm],
        out_specs=(vmem, vmem, vmem),
        scratch_shapes=[
            pltpu.VMEM((4, NZ, 128), f32),
            pltpu.VMEM((4, NZ, 128), f32),
            pltpu.VMEM((NZ, 2, 3, 64, 128), bf16),
            pltpu.VMEM((2, 3, 128, 128), f32),
            pltpu.VMEM((512, 768), bf16),
            pltpu.VMEM((512, 768), bf16),
            pltpu.VMEM((2, 4, 4, 64, 128), f32),
            pltpu.VMEM((4, 4, 64, 128), f32),
            pltpu.VMEM((4, 64, 128), f32),
            pltpu.VMEM((4, 3, 64, 128), bf16),
            pltpu.VMEM((4, 3, 64, 128), bf16),
            pltpu.VMEM((4, 64, 128), bf16),
            pltpu.VMEM((4, 8, 64, 128), bf16),
            pltpu.VMEM(perams.shape, bf16),
            pltpu.VMEM((3, 64, 128), f32),
            pltpu.VMEM((4096, 128), f32),
            pltpu.VMEM((128, 128), f32),
            pltpu.SMEM((3, 8), jnp.int32),
            pltpu.SMEM((4,), jnp.int32),
            pltpu.SMEM((2, 2, 3), jnp.int32),
            dma((3,)), dma(()), dma(()), dma((NZ, 2)), dma(()), dma((4,)), dma(()), dma((4,)),
            dma(()), dma((4, 3)), dma(()), dma((4,)), dma(()), dma(()), dma(()),
        ],
        compiler_params=pltpu.CompilerParams(
            collective_id=0, has_side_effects=True, vmem_limit_bytes=20 << 20
        ),
    )(*[pltpu.with_memory_space_constraint(value, pltpu.HBM) for value in (vecs, momenta, sources, spins, perams)])


def contract_kernel(rows_ref, second_op_ref, third_op_ref, out_ref, second):
    keep = lax.broadcasted_iota(jnp.int32, (64, 128), 1) < 64
    for which in range(PER_STEP):
        kreal, kimag = second_op_ref[which, 0], second_op_ref[which, 1]
        operator = jnp.concatenate(
            [jnp.concatenate([kreal, kimag], axis=1), jnp.concatenate([-kimag, kreal], axis=1)], axis=0
        )
        product = jnp.dot(rows_ref[which], operator, preferred_element_type=jnp.float32)
        for part in range(2):
            second[which, part] = product[:, part * 128 : (part + 1) * 128]
    for which in range(PER_STEP):
        columns = []
        for i in range(8):
            parts = []
            for part in range(2):
                straight = second[which, part, pl.ds(i, 32, stride=8), :]
                parts += [straight, pltpu.roll(straight, 64, 1)]
            columns.append(jnp.concatenate(parts, axis=0).astype(jnp.bfloat16))
        both = jnp.dot(third_op_ref[which], jnp.concatenate(columns, axis=1), preferred_element_type=jnp.float32)
        for i in range(8):
            lanes = slice(i * 128, (i + 1) * 128)
            out_ref[which * 8 + i] = jnp.where(keep, both[:64, lanes], both[64:, lanes])


def last_contractions(rows, second_op, third_op):
    return pl.pallas_call(
        contract_kernel,
        grid=(8 // PER_STEP,),
        out_shape=jax.ShapeDtypeStruct((64, 64, 128), jnp.float32),
        in_specs=[
            pl.BlockSpec((PER_STEP, 256, 256), lambda s: (s, 0, 0)),
            pl.BlockSpec((PER_STEP, 2, 128, 128), lambda s: (s, 0, 0, 0)),
            pl.BlockSpec((PER_STEP, 128, 128), lambda s: (s, 0, 0)),
        ],
        out_specs=pl.BlockSpec((8 * PER_STEP, 64, 128), lambda s: (s, 0, 0)),
        scratch_shapes=[pltpu.VMEM((PER_STEP, 2, 256, 128), jnp.float32)],
        compiler_params=pltpu.CompilerParams(
            dimension_semantics=("arbitrary",), vmem_limit_bytes=16 << 20
        ),
    )(rows, second_op, third_op)


def on_device(eigvecs, momenta, perams, sources, spins):
    operands = first_contraction(
        eigvecs[0], jnp.transpose(momenta), sources, jnp.transpose(spins, (0, 2, 1)), perams[0]
    )
    result = last_contractions(*operands)
    result = jnp.transpose(result.reshape(64, 32, 2, 128), (0, 2, 1, 3))
    return result.reshape(1, 4, 2, 8, 2, 4096)


def solution(mesh):
    placed = (
        P("tpair", None, None, None, "space"),
        P(),
        P("tpair", None, None, None, None),
        P(),
        P(),
    )
    return jax.shard_map(
        on_device,
        mesh=mesh,
        in_specs=placed,
        out_specs=P("tpair", None, None, "space", None, None),
        check_vma=False,
    )
```

```python
import functools

import jax
import jax.numpy as jnp
from jax import lax
from jax.experimental import pallas as pl
from jax.experimental.pallas import tpu as pltpu
from jax.sharding import PartitionSpec as P

LEXT = 64
TWO_PI = 6.283185307179586
MESH = pl.DeviceIdType.MESH

NX, NZ, NC = 4, 8, 2
NY = 4
HALF = NZ // 2


def place():
    index = lax.axis_index("space")
    return lax.div(index, NZ * NC), lax.rem(lax.div(index, NC), NZ), lax.rem(index, NC)


def at_space(x, z, c):
    return {"space": (x * NZ + z) * NC + c}


def elemental_kernel(
    vec_ref, mom_hbm, sources_hbm, spins_hbm, per_ref, rows_ref, second_op_ref, third_op_ref,
    cosines, sines, fields, vfloat, left, right, total, core_in, own_sum, outbox, inbox, chunk, all_chunks,
    arrived, wide, full, first_op, mom_ref, sources_ref, spins_ref, small_sem, own_sem, ring_send, ring_recv, core_send, core_recv, sum_send, sum_recv,
    share_send, share_recv, swap_send, swap_recv, per_send, per_recv, per_own,
):
    own = pltpu.make_async_copy(vec_ref, fields.at[0], own_sem)
    own.start()
    small = [
        pltpu.make_async_copy(mom_hbm, mom_ref, small_sem.at[0]),
        pltpu.make_async_copy(sources_hbm, sources_ref, small_sem.at[1]),
        pltpu.make_async_copy(spins_hbm, spins_ref, small_sem.at[2]),
    ]
    for copy in small:
        copy.start()
    x, z, c = place()
    y = lax.axis_index("tpair")
    zhalf, zz = lax.div(z, HALF), lax.rem(z, HALF)
    slot_q = zz * NC + c
    on_right = at_space(x, lax.rem(z + 1, NZ), c)
    on_left = at_space(x, lax.rem(z + NZ - 1, NZ), c)
    partner = at_space(x, z, 1 - c)
    across = [at_space(lax.rem(x + step, NX), z, c) for step in range(1, NX)]
    along = [at_space(x, zhalf * HALF + lax.rem(zz + step, HALF), c) for step in range(1, HALF)]
    sinks = [{"tpair": lax.rem(y + step, NY)} for step in range(1, NY)]

    barrier = pltpu.get_barrier_semaphore()
    greeted = [on_right, on_left, partner] + across + along + sinks
    for target in greeted:
        pl.semaphore_signal(barrier, inc=1, device_id=target, device_id_type=MESH)
    pl.semaphore_wait(barrier, len(greeted))
    own.wait()

    def remote(source, target, send_sem, recv_sem, device):
        return pltpu.make_async_remote_copy(
            src_ref=source, dst_ref=target, send_sem=send_sem, recv_sem=recv_sem,
            device_id=device, device_id_type=MESH,
        )

    def ring_copy(rel, piece, rightward):
        there = (rel + NZ - 1) % NZ if rightward else (rel + 1) % NZ
        return remote(
            fields.at[rel, piece // 3, piece % 3], fields.at[there, piece // 3, piece % 3], ring_send, ring_recv.at[there, piece],
            on_right if rightward else on_left,
        )

    for piece in range(6):
        ring_copy(0, piece, True).start()
        ring_copy(0, piece, False).start()

    for step in range(1, NY):
        remote(per_ref.at[lax.rem(y + step, NY)], arrived.at[y], per_send, per_recv, sinks[step - 1]).start()
    per_local = pltpu.make_async_copy(per_ref.at[y], arrived.at[y], per_own)
    per_local.start()

    def relay(step):
        for piece in range(6):
            if step < HALF or piece < 3:
                rel = NZ - step
                remote(fields.at[rel, piece // 3, piece % 3], fields.at[rel, piece // 3, piece % 3], ring_send, ring_recv.at[rel, piece], on_right).wait_recv()
                if step < HALF - 1 or (step == HALF - 1 and piece < 3):
                    ring_copy(rel, piece, True).start()
            if step < HALF or piece >= 3:
                rel = step
                remote(fields.at[rel, piece // 3, piece % 3], fields.at[rel, piece // 3, piece % 3], ring_send, ring_recv.at[rel, piece], on_left).wait_recv()
                if step < HALF - 1 or (step == HALF - 1 and piece >= 3):
                    ring_copy(rel, piece, False).start()

    for copy in small:
        copy.wait()

    row = lax.broadcasted_iota(jnp.int32, (NZ, 128), 0)
    lane = lax.broadcasted_iota(jnp.int32, (NZ, 128), 1)
    sites = ((x * NZ + ((z + row) & (NZ - 1))) * NC + c) * 128 + lane
    xs, ys, zs = sites & (LEXT - 1), (sites >> 6) & (LEXT - 1), sites >> 12
    factor = lax.rsqrt(jnp.float32(24.0 * 128 * NX * NZ * NC))
    for mom in range(4):
        mine = 2 * mom + zhalf
        turns = mom_ref[0, mine] * xs + mom_ref[1, mine] * ys + mom_ref[2, mine] * zs
        angle = (turns & (LEXT - 1)).astype(jnp.float32) * (TWO_PI / LEXT)
        cosines[mom] = jnp.cos(angle) * factor
        sines[mom] = jnp.sin(angle) * factor

    total[...] = jnp.zeros_like(total)

    def contract(rel):
        for part in range(2):
            for colour in range(3):
                values = fields[rel, part, colour].astype(jnp.float32)
                vfloat[part, colour, 0:64] = values
                vfloat[part, colour, 64:128] = values
        for colour in range(3):
            nxt, aft = (colour + 1) % 3, (colour + 2) % 3
            for odd in range(2):
                rows = pl.ds(odd, 32, stride=2)
                lrn, lin = vfloat[0, nxt, rows], vfloat[1, nxt, rows]
                lra, lia = vfloat[0, aft, rows], vfloat[1, aft, rows]
                for core in range(2):
                    for group in range(4):
                        rows = pl.ds(1 + zz * NC + core + 8 * group + odd, 32, stride=2)
                        rrn, rin = vfloat[0, nxt, rows], vfloat[1, nxt, rows]
                        rra, ria = vfloat[0, aft, rows], vfloat[1, aft, rows]
                        real = lrn * rra - lin * ria - (lra * rrn - lia * rin)
                        imag = lrn * ria + lin * rra - (lra * rin + lia * rrn)
                        where = pl.ds(core * 256 + group * 64 + odd * 32, 32)
                        left[where, colour * 128 : (colour + 1) * 128] = real.astype(jnp.bfloat16)
                        left[where, (3 + colour) * 128 : (4 + colour) * 128] = imag.astype(jnp.bfloat16)
        at = pl.ds(rel, 1)
        for colour in range(3):
            for odd in range(2):
                rows = pl.ds(odd, 32, stride=2)
                vr, vi = vfloat[0, colour, rows], vfloat[1, colour, rows]
                for mom in range(4):
                    cosine, sine = cosines[mom, at, :], sines[mom, at, :]
                    pr = (cosine * vr + sine * vi).astype(jnp.bfloat16)
                    pi = (cosine * vi - sine * vr).astype(jnp.bfloat16)
                    upper, lower = pl.ds(mom * 128 + odd * 32, 32), pl.ds(mom * 128 + 64 + odd * 32, 32)
                    first, second = pl.ds(colour * 128, 128), pl.ds((3 + colour) * 128, 128)
                    right[upper, first] = pr
                    right[upper, second] = -pi
                    right[lower, first] = pi
                    right[lower, second] = pr
        product = lax.dot_general(
            left[...], right[...], (((1,), (1,)), ((), ())), preferred_element_type=jnp.float32
        )
        for core in range(2):
            for group in range(4):
                at = core * 256 + group * 64
                for mom in range(4):
                    total[core, group, mom] += product[at : at + 64, mom * 128 : (mom + 1) * 128]

    def body(n, carry):
        contract(jnp.where(n % 2 == 1, NZ - (n + 1) // 2, n // 2))
        for after, step in ((0, 1), (1, 2), (3, 3), (5, 4)):
            pl.when(n == after)(functools.partial(relay, step))
        return carry

    lax.fori_loop(0, NZ, body, 0)

    for group in range(4):
        remote(total.at[1 - c, group], core_in.at[group], core_send, core_recv.at[group], partner).start()

    def share_arrival(group, step):
        owner = lax.rem(zz + HALF - step, HALF) * NC + c
        return remote(
            chunk.at[group], all_chunks.at[group, owner], share_send, share_recv.at[group, step - 1], along[step - 1]
        )

    def swap_copy(group, step):
        owner = lax.rem(zz + HALF - step, HALF) * NC + c
        return remote(
            chunk.at[group] if step == 0 else all_chunks.at[group, owner],
            all_chunks.at[group, owner], swap_send, swap_recv.at[group], partner,
        )

    low = lax.broadcasted_iota(jnp.int32, (32, 128), 1) < 64
    even = lax.broadcasted_iota(jnp.int32, (32, 128), 1) % 2 == 0
    row = lax.broadcasted_iota(jnp.int32, (16, 128), 0)
    lane = lax.broadcasted_iota(jnp.int32, (16, 128), 1)
    rank = lax.axis_index("space") % 8
    pick = (lane == (row // 8) * 64 + rank * 8 + row % 8).astype(jnp.float32).astype(jnp.bfloat16)
    row = lax.broadcasted_iota(jnp.int32, (128, 128), 0)
    lane = lax.broadcasted_iota(jnp.int32, (128, 128), 1)
    wanted = (row % 2) * 64 + 2 * (row % 64 // 2) + row // 64
    order = (lane == wanted).astype(jnp.float32).astype(jnp.bfloat16)

    def rolled(value):
        return pltpu.roll(value, 64, 1)

    def tau(which, quark):
        source, comb = sources_ref[which // 2], which % 2
        spin = spins_ref[comb, 0, quark] * 4 + spins_ref[comb, 1, quark]
        flat = arrived[source, spin].astype(jnp.float32)
        for pair in range(32):
            wide[quark, 2 * pair : 2 * pair + 2, :] = flat[:, pair * 128 : (pair + 1) * 128]
        return wide[quark, pl.ds(0, 32, stride=2), :], wide[quark, pl.ds(1, 32, stride=2), :]

    def both_of_pair(value):
        turned, zero = rolled(value), jnp.zeros_like(value)
        return jnp.concatenate(
            [
                jnp.where(low, value, zero),
                jnp.where(low, turned, zero),
                jnp.where(low, zero, turned),
                jnp.where(low, zero, value),
            ],
            axis=0,
        ).astype(jnp.bfloat16)

    def arranged(upper, lower):
        uturn, lturn = rolled(upper), rolled(lower)
        straight = jnp.where(low, jnp.where(even, upper, uturn), jnp.where(even, lturn, lower))
        turned = jnp.where(low, jnp.where(even, uturn, upper), jnp.where(even, lower, lturn))
        return [straight, turned]

    def operators(which, carry):
        real, imag = tau(which, 0)
        upper = jnp.concatenate([real, rolled(real), -imag, -rolled(imag)], axis=0)
        lower = jnp.concatenate([rolled(imag), imag, rolled(real), real], axis=0)
        lanes = lax.broadcasted_iota(jnp.int32, (128, 128), 1)
        picked = lax.dot_general(
            pick,
            jnp.where(lanes < 64, upper, lower).astype(jnp.bfloat16),
            (((1,), (1,)), ((), ())),
            preferred_element_type=jnp.float32,
        )
        for part in range(2):
            at = pl.ds(pl.multiple_of(part * 64 + which * 8, 8), 8)
            first_op[at, :] = picked[part * 8 : part * 8 + 8]
        real, imag = tau(which, 2)
        second_op_ref[which, 0] = both_of_pair(real)
        second_op_ref[which, 1] = both_of_pair(imag)
        real, imag = tau(which, 1)
        operator = jnp.concatenate(arranged(real, imag) + arranged(-imag, real), axis=0)
        third_op_ref[which] = lax.dot_general(
            order, operator.astype(jnp.bfloat16), (((1,), (1,)), ((), ())),
            preferred_element_type=jnp.float32,
        ).astype(jnp.bfloat16)
        return carry

    for group in range(4):
        remote(core_in.at[group], core_in.at[group], core_send, core_recv.at[group], partner).wait_recv()
        for step in (2, 1, 3):
            mom = lax.rem(x + step, NX)
            outbox[group, step - 1] = (total[c, group, mom] + core_in[group, mom]).astype(jnp.bfloat16)
            remote(
                outbox.at[group, step - 1], inbox.at[group, step - 1], sum_send, sum_recv.at[group], across[step - 1]
            ).start()
        own_sum[group] = total[c, group, x] + core_in[group, x]

    per_local.wait()
    remote(per_ref.at[0:3], arrived.at[0:3], per_send, per_recv, sinks[0]).wait()
    lax.fori_loop(0, 4, operators, 0)

    for group in range(4):
        remote(inbox.at[group], inbox.at[group], sum_send, sum_recv.at[group], across[0]).wait_recv()
        summed = own_sum[group]
        for step in range(3):
            summed = summed + inbox[group, step].astype(jnp.float32)
        chunk[group] = summed.astype(jnp.bfloat16)
        for step in (3, 2, 1):
            remote(
                chunk.at[group], all_chunks.at[group, slot_q], share_send, share_recv.at[group, step - 1], along[step - 1]
            ).start()
        swap_copy(group, 0).start()
        all_chunks[group, slot_q] = chunk[group]

    lax.fori_loop(4, 8, operators, 0)
    full[pl.ds(0, 32, stride=129), :] = jnp.zeros((32, 128), jnp.float32)
    full[pl.ds(96, 32, stride=129), :] = jnp.zeros((32, 128), jnp.float32)

    def onward(group):
        for step in (1, 3, 2):
            share_arrival(group, step).wait_recv()
            swap_copy(group, step).start()

    def expand(group):
        remote(chunk, chunk, swap_send, swap_recv.at[group], partner).wait_recv()
        for q in range(8):
            d = 1 + q + 8 * group
            for odd in range(2):
                piece = all_chunks[group, q, odd * 32 : odd * 32 + 32, :].astype(jnp.float32)
                kodd = (odd + d) % 2
                e = (odd + d - kodd) // 2
                base = odd * 64 + kodd * 32 + e
                full[pl.ds(base, 32 - e, stride=129), :] = piece[: 32 - e]
                if e:
                    full[pl.ds(129 * (32 - e) + base - 32, e, stride=129), :] = piece[32 - e :]
                if d < 32:
                    base = 128 * e + kodd * 64 + odd * 32
                    full[pl.ds(base, 32 - e, stride=129), :] = -piece[: 32 - e]
                    if e:
                        full[pl.ds(129 * (32 - e) + base - 4096, e, stride=129), :] = -piece[32 - e :]

    onward(0)
    onward(1)
    expand(0)
    onward(2)
    expand(1)
    onward(3)
    expand(2)
    expand(3)

    operator = first_op[...].astype(jnp.bfloat16)
    for two in range(16):
        block = full[two * 256 : (two + 1) * 256, :].astype(jnp.bfloat16)
        first = lax.dot_general(
            operator, block, (((1,), (1,)), ((), ())), preferred_element_type=jnp.float32
        )
        for part in range(2):
            for which in range(8):
                at = part * 64 + which * 8
                piece = jnp.concatenate([first[at : at + 8, :128], first[at : at + 8, 128:]], axis=0)
                rows_ref[which, two * 16 : two * 16 + 16, part * 128 : (part + 1) * 128] = piece.astype(jnp.bfloat16)

    remote(fields.at[0:7], fields.at[0:7], ring_send, ring_recv.at[0, 0], on_right).wait_send()
    remote(core_in, core_in, core_send, core_recv.at[0], partner).wait_send()
    remote(outbox, inbox, sum_send, sum_recv.at[0], across[0]).wait_send()
    remote(outbox, inbox, share_send, share_recv.at[0, 0], along[0]).wait_send()
    remote(all_chunks.at[0:2], all_chunks.at[0:2], swap_send, swap_recv.at[0], partner).wait_send()


def first_contraction(vecs, momenta, sources, spins, perams):
    vmem = pl.BlockSpec(memory_space=pltpu.VMEM)
    hbm = pl.BlockSpec(memory_space=pltpu.HBM)
    dma, bf16, f32 = pltpu.SemaphoreType.DMA, jnp.bfloat16, jnp.float32
    return pl.pallas_call(
        elemental_kernel,
        out_shape=(
            jax.ShapeDtypeStruct((8, 256, 256), bf16),
            jax.ShapeDtypeStruct((8, 2, 128, 128), bf16),
            jax.ShapeDtypeStruct((8, 128, 128), bf16),
        ),
        in_specs=[hbm, hbm, hbm, hbm, hbm],
        out_specs=(vmem, vmem, vmem),
        scratch_shapes=[
            pltpu.VMEM((4, NZ, 128), f32),
            pltpu.VMEM((4, NZ, 128), f32),
            pltpu.VMEM((NZ, 2, 3, 64, 128), bf16),
            pltpu.VMEM((2, 3, 128, 128), f32),
            pltpu.VMEM((512, 768), bf16),
            pltpu.VMEM((512, 768), bf16),
            pltpu.VMEM((2, 4, 4, 64, 128), f32),
            pltpu.VMEM((4, 4, 64, 128), f32),
            pltpu.VMEM((4, 64, 128), f32),
            pltpu.VMEM((4, 3, 64, 128), bf16),
            pltpu.VMEM((4, 3, 64, 128), bf16),
            pltpu.VMEM((4, 64, 128), bf16),
            pltpu.VMEM((4, 8, 64, 128), bf16),
            pltpu.VMEM(perams.shape, bf16),
            pltpu.VMEM((3, 64, 128), f32),
            pltpu.VMEM((4096, 128), f32),
            pltpu.VMEM((128, 128), f32),
            pltpu.SMEM((3, 8), jnp.int32),
            pltpu.SMEM((4,), jnp.int32),
            pltpu.SMEM((2, 2, 3), jnp.int32),
            dma((3,)), dma(()), dma(()), dma((NZ, 6)), dma(()), dma((4,)), dma(()), dma((4,)),
            dma(()), dma((4, 3)), dma(()), dma((4,)), dma(()), dma(()), dma(()),
        ],
        compiler_params=pltpu.CompilerParams(
            collective_id=0, has_side_effects=True, vmem_limit_bytes=20 << 20
        ),
    )(*[pltpu.with_memory_space_constraint(value, pltpu.HBM) for value in (vecs, momenta, sources, spins, perams)])


def contract_kernel(rows_ref, second_op_ref, third_op_ref, out_ref, second, held, out_sem):
    keep = lax.broadcasted_iota(jnp.int32, (64, 128), 1) < 64
    copies = []
    for which in range(8):
        kreal, kimag = second_op_ref[which, 0], second_op_ref[which, 1]
        operator = jnp.concatenate(
            [jnp.concatenate([kreal, kimag], axis=1), jnp.concatenate([-kimag, kreal], axis=1)], axis=0
        )
        product = jnp.dot(rows_ref[which], operator, preferred_element_type=jnp.float32)
        for part in range(2):
            second[which, part] = product[:, part * 128 : (part + 1) * 128]
    for which in range(8):
        columns = []
        for i in range(8):
            parts = []
            for part in range(2):
                straight = second[which, part, pl.ds(i, 32, stride=8), :]
                parts += [straight, pltpu.roll(straight, 64, 1)]
            columns.append(jnp.concatenate(parts, axis=0).astype(jnp.bfloat16))
        both = jnp.dot(third_op_ref[which], jnp.concatenate(columns, axis=1), preferred_element_type=jnp.float32)
        for i in range(8):
            lanes = slice(i * 128, (i + 1) * 128)
            held[which * 8 + i] = jnp.where(keep, both[:64, lanes], both[64:, lanes])
        here = pl.ds(which * 8, 8)
        copies.append(pltpu.make_async_copy(held.at[here], out_ref.at[here], out_sem.at[which]))
        copies[-1].start()
    for copy in copies:
        copy.wait()


def last_contractions(rows, second_op, third_op):
    vmem = pl.BlockSpec(memory_space=pltpu.VMEM)
    return pl.pallas_call(
        contract_kernel,
        out_shape=jax.ShapeDtypeStruct((64, 64, 128), jnp.float32),
        in_specs=[vmem, vmem, vmem],
        out_specs=pl.BlockSpec(memory_space=pltpu.HBM),
        scratch_shapes=[
            pltpu.VMEM((8, 2, 256, 128), jnp.float32),
            pltpu.VMEM((64, 64, 128), jnp.float32),
            pltpu.SemaphoreType.DMA((8,)),
        ],
        compiler_params=pltpu.CompilerParams(vmem_limit_bytes=16 << 20),
    )(rows, second_op, third_op)


def on_device(eigvecs, momenta, perams, sources, spins):
    operands = first_contraction(
        eigvecs[0], jnp.transpose(momenta), sources, jnp.transpose(spins, (0, 2, 1)), perams[0]
    )
    result = last_contractions(*operands)
    result = jnp.transpose(result.reshape(64, 32, 2, 128), (0, 2, 1, 3))
    return result.reshape(1, 4, 2, 8, 2, 4096)


def solution(mesh):
    placed = (
        P("tpair", None, None, None, "space"),
        P(),
        P("tpair", None, None, None, None),
        P(),
        P(),
    )
    return jax.shard_map(
        on_device,
        mesh=mesh,
        in_specs=placed,
        out_specs=P("tpair", None, None, "space", None, None),
        check_vma=False,
    )
```

```python
import functools

import jax
import jax.numpy as jnp
from jax import lax
from jax.experimental import pallas as pl
from jax.experimental.pallas import tpu as pltpu
from jax.sharding import PartitionSpec as P

LEXT = 64
TWO_PI = 6.283185307179586
MESH = pl.DeviceIdType.MESH

NX, NZ, NC = 4, 8, 2
NY = 4
HALF = NZ // 2


def place():
    index = lax.axis_index("space")
    return lax.div(index, NZ * NC), lax.rem(lax.div(index, NC), NZ), lax.rem(index, NC)


def at_space(x, z, c):
    return {"space": (x * NZ + z) * NC + c}


def elemental_kernel(
    vec_ref, mom_hbm, sources_hbm, spins_hbm, per_ref, rows_ref, second_op_ref, third_op_ref,
    cosines, sines, fields, vfloat, left, right, total, core_in, own_sum, outbox, inbox, chunk, all_chunks,
    arrived, wide, full, first_op, mom_ref, sources_ref, spins_ref, small_sem, own_sem, ring_send, ring_recv, core_send, core_recv, sum_send, sum_recv,
    share_send, share_recv, swap_send, swap_recv, per_send, per_recv, per_own,
):
    own = pltpu.make_async_copy(vec_ref, fields.at[0], own_sem)
    own.start()
    small = [
        pltpu.make_async_copy(mom_hbm, mom_ref, small_sem.at[0]),
        pltpu.make_async_copy(sources_hbm, sources_ref, small_sem.at[1]),
        pltpu.make_async_copy(spins_hbm, spins_ref, small_sem.at[2]),
    ]
    for copy in small:
        copy.start()
    x, z, c = place()
    y = lax.axis_index("tpair")
    zhalf, zz = lax.div(z, HALF), lax.rem(z, HALF)
    slot_q = zz * NC + c
    on_right = at_space(x, lax.rem(z + 1, NZ), c)
    on_left = at_space(x, lax.rem(z + NZ - 1, NZ), c)
    partner = at_space(x, z, 1 - c)
    across = [at_space(lax.rem(x + step, NX), z, c) for step in range(1, NX)]
    along = [at_space(x, zhalf * HALF + lax.rem(zz + step, HALF), c) for step in range(1, HALF)]
    sinks = [{"tpair": lax.rem(y + step, NY)} for step in range(1, NY)]

    barrier = pltpu.get_barrier_semaphore()
    greeted = [on_right, on_left, partner] + across + along + sinks
    for target in greeted:
        pl.semaphore_signal(barrier, inc=1, device_id=target, device_id_type=MESH)
    pl.semaphore_wait(barrier, len(greeted))
    own.wait()

    def remote(source, target, send_sem, recv_sem, device):
        return pltpu.make_async_remote_copy(
            src_ref=source, dst_ref=target, send_sem=send_sem, recv_sem=recv_sem,
            device_id=device, device_id_type=MESH,
        )

    def ring_copy(rel, piece, rightward):
        there = (rel + NZ - 1) % NZ if rightward else (rel + 1) % NZ
        return remote(
            fields.at[rel, piece // 3, piece % 3], fields.at[there, piece // 3, piece % 3], ring_send, ring_recv.at[there, piece],
            on_right if rightward else on_left,
        )

    for piece in range(6):
        ring_copy(0, piece, True).start()
        ring_copy(0, (piece + 3) % 6, False).start()

    for step in range(1, NY):
        remote(per_ref.at[lax.rem(y + step, NY)], arrived.at[y], per_send, per_recv, sinks[step - 1]).start()
    per_local = pltpu.make_async_copy(per_ref.at[y], arrived.at[y], per_own)
    per_local.start()

    def relay(step, late):
        for count in range(3):
            for rightward in (True, False):
                piece = count + 3 * (late if rightward else 1 - late)
                if step == HALF and late:
                    continue
                rel = NZ - step if rightward else step
                here = fields.at[rel, piece // 3, piece % 3]
                remote(here, here, ring_send, ring_recv.at[rel, piece], on_right if rightward else on_left).wait_recv()
                if step < HALF - 1 or (step == HALF - 1 and not late):
                    ring_copy(rel, piece, rightward).start()

    for copy in small:
        copy.wait()

    row = lax.broadcasted_iota(jnp.int32, (NZ, 128), 0)
    lane = lax.broadcasted_iota(jnp.int32, (NZ, 128), 1)
    sites = ((x * NZ + ((z + row) & (NZ - 1))) * NC + c) * 128 + lane
    xs, ys, zs = sites & (LEXT - 1), (sites >> 6) & (LEXT - 1), sites >> 12
    factor = lax.rsqrt(jnp.float32(24.0 * 128 * NX * NZ * NC))
    for mom in range(4):
        mine = 2 * mom + zhalf
        turns = mom_ref[0, mine] * xs + mom_ref[1, mine] * ys + mom_ref[2, mine] * zs
        angle = (turns & (LEXT - 1)).astype(jnp.float32) * (TWO_PI / LEXT)
        cosines[mom] = jnp.cos(angle) * factor
        sines[mom] = jnp.sin(angle) * factor

    total[...] = jnp.zeros_like(total)

    def contract(rel):
        for part in range(2):
            for colour in range(3):
                values = fields[rel, part, colour].astype(jnp.float32)
                vfloat[part, colour, 0:64] = values
                vfloat[part, colour, 64:128] = values
        at = pl.ds(rel, 1)
        for colour in range(3):
            for odd in range(2):
                rows = pl.ds(odd, 32, stride=2)
                vr, vi = vfloat[0, colour, rows], vfloat[1, colour, rows]
                for mom in range(4):
                    cosine, sine = cosines[mom, at, :], sines[mom, at, :]
                    pr = (cosine * vr + sine * vi).astype(jnp.bfloat16)
                    pi = (cosine * vi - sine * vr).astype(jnp.bfloat16)
                    upper, lower = pl.ds(mom * 128 + odd * 32, 32), pl.ds(mom * 128 + 64 + odd * 32, 32)
                    first, second = pl.ds(colour * 128, 128), pl.ds((3 + colour) * 128, 128)
                    right[upper, first] = pr
                    right[upper, second] = -pi
                    right[lower, first] = pi
                    right[lower, second] = pr
        for colour in range(3):
            nxt, aft = (colour + 1) % 3, (colour + 2) % 3
            for odd in range(2):
                rows = pl.ds(odd, 32, stride=2)
                lrn, lin = vfloat[0, nxt, rows], vfloat[1, nxt, rows]
                lra, lia = vfloat[0, aft, rows], vfloat[1, aft, rows]
                for core in range(2):
                    for group in range(4):
                        rows = pl.ds(1 + zz * NC + core + 8 * group + odd, 32, stride=2)
                        rrn, rin = vfloat[0, nxt, rows], vfloat[1, nxt, rows]
                        rra, ria = vfloat[0, aft, rows], vfloat[1, aft, rows]
                        real = lrn * rra - lin * ria - (lra * rrn - lia * rin)
                        imag = lrn * ria + lin * rra - (lra * rin + lia * rrn)
                        where = pl.ds(core * 256 + group * 64 + odd * 32, 32)
                        left[where, colour * 128 : (colour + 1) * 128] = real.astype(jnp.bfloat16)
                        left[where, (3 + colour) * 128 : (4 + colour) * 128] = imag.astype(jnp.bfloat16)
        product = lax.dot_general(
            left[...], right[...], (((1,), (1,)), ((), ())), preferred_element_type=jnp.float32
        )
        for core in range(2):
            for group in range(4):
                at = core * 256 + group * 64
                for mom in range(4):
                    total[core, group, mom] += product[at : at + 64, mom * 128 : (mom + 1) * 128]

    def body(n, carry):
        contract(jnp.where(n % 2 == 1, NZ - (n + 1) // 2, n // 2))
        for after, step, late in ((0, 1, 0), (0, 1, 1), (1, 2, 0), (1, 2, 1), (3, 3, 0), (4, 3, 1), (6, 4, 0)):
            pl.when(n == after)(functools.partial(relay, step, late))
        return carry

    lax.fori_loop(0, NZ, body, 0)

    for group in range(4):
        remote(total.at[1 - c, group], core_in.at[group], core_send, core_recv.at[group], partner).start()

    def share_arrival(group, step):
        owner = lax.rem(zz + HALF - step, HALF) * NC + c
        return remote(
            chunk.at[group], all_chunks.at[group, owner], share_send, share_recv.at[group, step - 1], along[step - 1]
        )

    def swap_copy(group, step):
        owner = lax.rem(zz + HALF - step, HALF) * NC + c
        return remote(
            chunk.at[group] if step == 0 else all_chunks.at[group, owner],
            all_chunks.at[group, owner], swap_send, swap_recv.at[group], partner,
        )

    low = lax.broadcasted_iota(jnp.int32, (32, 128), 1) < 64
    even = lax.broadcasted_iota(jnp.int32, (32, 128), 1) % 2 == 0
    row = lax.broadcasted_iota(jnp.int32, (16, 128), 0)
    lane = lax.broadcasted_iota(jnp.int32, (16, 128), 1)
    rank = lax.axis_index("space") % 8
    pick = (lane == (row // 8) * 64 + rank * 8 + row % 8).astype(jnp.float32).astype(jnp.bfloat16)
    row = lax.broadcasted_iota(jnp.int32, (128, 128), 0)
    lane = lax.broadcasted_iota(jnp.int32, (128, 128), 1)
    wanted = (row % 2) * 64 + 2 * (row % 64 // 2) + row // 64
    order = (lane == wanted).astype(jnp.float32).astype(jnp.bfloat16)

    def rolled(value):
        return pltpu.roll(value, 64, 1)

    def tau(which, quark):
        source, comb = sources_ref[which // 2], which % 2
        spin = spins_ref[comb, 0, quark] * 4 + spins_ref[comb, 1, quark]
        flat = arrived[source, spin].astype(jnp.float32)
        for pair in range(32):
            wide[quark, 2 * pair : 2 * pair + 2, :] = flat[:, pair * 128 : (pair + 1) * 128]
        return wide[quark, pl.ds(0, 32, stride=2), :], wide[quark, pl.ds(1, 32, stride=2), :]

    def both_of_pair(value):
        turned, zero = rolled(value), jnp.zeros_like(value)
        return jnp.concatenate(
            [
                jnp.where(low, value, zero),
                jnp.where(low, turned, zero),
                jnp.where(low, zero, turned),
                jnp.where(low, zero, value),
            ],
            axis=0,
        ).astype(jnp.bfloat16)

    def arranged(upper, lower):
        uturn, lturn = rolled(upper), rolled(lower)
        straight = jnp.where(low, jnp.where(even, upper, uturn), jnp.where(even, lturn, lower))
        turned = jnp.where(low, jnp.where(even, uturn, upper), jnp.where(even, lower, lturn))
        return [straight, turned]

    def operators(which, carry):
        real, imag = tau(which, 0)
        upper = jnp.concatenate([real, rolled(real), -imag, -rolled(imag)], axis=0)
        lower = jnp.concatenate([rolled(imag), imag, rolled(real), real], axis=0)
        lanes = lax.broadcasted_iota(jnp.int32, (128, 128), 1)
        picked = lax.dot_general(
            pick,
            jnp.where(lanes < 64, upper, lower).astype(jnp.bfloat16),
            (((1,), (1,)), ((), ())),
            preferred_element_type=jnp.float32,
        )
        for part in range(2):
            at = pl.ds(pl.multiple_of(part * 64 + which * 8, 8), 8)
            first_op[at, :] = picked[part * 8 : part * 8 + 8]
        real, imag = tau(which, 2)
        second_op_ref[which, 0] = both_of_pair(real)
        second_op_ref[which, 1] = both_of_pair(imag)
        real, imag = tau(which, 1)
        operator = jnp.concatenate(arranged(real, imag) + arranged(-imag, real), axis=0)
        third_op_ref[which] = lax.dot_general(
            order, operator.astype(jnp.bfloat16), (((1,), (1,)), ((), ())),
            preferred_element_type=jnp.float32,
        ).astype(jnp.bfloat16)
        return carry

    for group in range(4):
        remote(core_in.at[group], core_in.at[group], core_send, core_recv.at[group], partner).wait_recv()
        for step in (2, 1, 3):
            mom = lax.rem(x + step, NX)
            outbox[group, step - 1] = (total[c, group, mom] + core_in[group, mom]).astype(jnp.bfloat16)
            remote(
                outbox.at[group, step - 1], inbox.at[group, step - 1], sum_send, sum_recv.at[group], across[step - 1]
            ).start()
        own_sum[group] = total[c, group, x] + core_in[group, x]

    per_local.wait()
    remote(per_ref.at[0:3], arrived.at[0:3], per_send, per_recv, sinks[0]).wait()
    lax.fori_loop(0, 4, operators, 0)

    for group in range(4):
        remote(inbox.at[group], inbox.at[group], sum_send, sum_recv.at[group], across[0]).wait_recv()
        summed = own_sum[group]
        for step in range(3):
            summed = summed + inbox[group, step].astype(jnp.float32)
        chunk[group] = summed.astype(jnp.bfloat16)
        for step in (3, 2, 1):
            remote(
                chunk.at[group], all_chunks.at[group, slot_q], share_send, share_recv.at[group, step - 1], along[step - 1]
            ).start()
        swap_copy(group, 0).start()
        all_chunks[group, slot_q] = chunk[group]

    lax.fori_loop(4, 8, operators, 0)
    full[pl.ds(0, 32, stride=129), :] = jnp.zeros((32, 128), jnp.float32)
    full[pl.ds(96, 32, stride=129), :] = jnp.zeros((32, 128), jnp.float32)

    def onward(group):
        for step in (1, 3, 2):
            share_arrival(group, step).wait_recv()
            swap_copy(group, step).start()

    def expand(group):
        remote(chunk, chunk, swap_send, swap_recv.at[group], partner).wait_recv()
        for q in range(8):
            d = 1 + q + 8 * group
            for odd in range(2):
                piece = all_chunks[group, q, odd * 32 : odd * 32 + 32, :].astype(jnp.float32)
                kodd = (odd + d) % 2
                e = (odd + d - kodd) // 2
                base = odd * 64 + kodd * 32 + e
                full[pl.ds(base, 32 - e, stride=129), :] = piece[: 32 - e]
                if e:
                    full[pl.ds(129 * (32 - e) + base - 32, e, stride=129), :] = piece[32 - e :]
                if d < 32:
                    base = 128 * e + kodd * 64 + odd * 32
                    full[pl.ds(base, 32 - e, stride=129), :] = -piece[: 32 - e]
                    if e:
                        full[pl.ds(129 * (32 - e) + base - 4096, e, stride=129), :] = -piece[32 - e :]

    onward(0)
    onward(1)
    expand(0)
    onward(2)
    expand(1)
    onward(3)
    expand(2)
    expand(3)

    operator = first_op[...].astype(jnp.bfloat16)
    for two in range(16):
        block = full[two * 256 : (two + 1) * 256, :].astype(jnp.bfloat16)
        first = lax.dot_general(
            operator, block, (((1,), (1,)), ((), ())), preferred_element_type=jnp.float32
        )
        for part in range(2):
            for which in range(8):
                at = part * 64 + which * 8
                piece = jnp.concatenate([first[at : at + 8, :128], first[at : at + 8, 128:]], axis=0)
                rows_ref[which, two * 16 : two * 16 + 16, part * 128 : (part + 1) * 128] = piece.astype(jnp.bfloat16)

    remote(fields.at[0:7], fields.at[0:7], ring_send, ring_recv.at[0, 0], on_right).wait_send()
    remote(core_in, core_in, core_send, core_recv.at[0], partner).wait_send()
    remote(outbox, inbox, sum_send, sum_recv.at[0], across[0]).wait_send()
    remote(outbox, inbox, share_send, share_recv.at[0, 0], along[0]).wait_send()
    remote(all_chunks.at[0:2], all_chunks.at[0:2], swap_send, swap_recv.at[0], partner).wait_send()


def first_contraction(vecs, momenta, sources, spins, perams):
    vmem = pl.BlockSpec(memory_space=pltpu.VMEM)
    hbm = pl.BlockSpec(memory_space=pltpu.HBM)
    dma, bf16, f32 = pltpu.SemaphoreType.DMA, jnp.bfloat16, jnp.float32
    return pl.pallas_call(
        elemental_kernel,
        out_shape=(
            jax.ShapeDtypeStruct((8, 256, 256), bf16),
            jax.ShapeDtypeStruct((8, 2, 128, 128), bf16),
            jax.ShapeDtypeStruct((8, 128, 128), bf16),
        ),
        in_specs=[hbm, hbm, hbm, hbm, hbm],
        out_specs=(vmem, vmem, vmem),
        scratch_shapes=[
            pltpu.VMEM((4, NZ, 128), f32),
            pltpu.VMEM((4, NZ, 128), f32),
            pltpu.VMEM((NZ, 2, 3, 64, 128), bf16),
            pltpu.VMEM((2, 3, 128, 128), f32),
            pltpu.VMEM((512, 768), bf16),
            pltpu.VMEM((512, 768), bf16),
            pltpu.VMEM((2, 4, 4, 64, 128), f32),
            pltpu.VMEM((4, 4, 64, 128), f32),
            pltpu.VMEM((4, 64, 128), f32),
            pltpu.VMEM((4, 3, 64, 128), bf16),
            pltpu.VMEM((4, 3, 64, 128), bf16),
            pltpu.VMEM((4, 64, 128), bf16),
            pltpu.VMEM((4, 8, 64, 128), bf16),
            pltpu.VMEM(perams.shape, bf16),
            pltpu.VMEM((3, 64, 128), f32),
            pltpu.VMEM((4096, 128), f32),
            pltpu.VMEM((128, 128), f32),
            pltpu.SMEM((3, 8), jnp.int32),
            pltpu.SMEM((4,), jnp.int32),
            pltpu.SMEM((2, 2, 3), jnp.int32),
            dma((3,)), dma(()), dma(()), dma((NZ, 6)), dma(()), dma((4,)), dma(()), dma((4,)),
            dma(()), dma((4, 3)), dma(()), dma((4,)), dma(()), dma(()), dma(()),
        ],
        compiler_params=pltpu.CompilerParams(
            collective_id=0, has_side_effects=True, vmem_limit_bytes=20 << 20
        ),
    )(*[pltpu.with_memory_space_constraint(value, pltpu.HBM) for value in (vecs, momenta, sources, spins, perams)])


def contract_kernel(rows_ref, second_op_ref, third_op_ref, out_ref, second, held, out_sem):
    keep = lax.broadcasted_iota(jnp.int32, (64, 128), 1) < 64
    copies = []
    for which in range(8):
        kreal, kimag = second_op_ref[which, 0], second_op_ref[which, 1]
        operator = jnp.concatenate(
            [jnp.concatenate([kreal, kimag], axis=1), jnp.concatenate([-kimag, kreal], axis=1)], axis=0
        )
        product = jnp.dot(rows_ref[which], operator, preferred_element_type=jnp.float32)
        for part in range(2):
            second[which, part] = product[:, part * 128 : (part + 1) * 128]
    for which in range(8):
        columns = []
        for i in range(8):
            parts = []
            for part in range(2):
                straight = second[which, part, pl.ds(i, 32, stride=8), :]
                parts += [straight, pltpu.roll(straight, 64, 1)]
            columns.append(jnp.concatenate(parts, axis=0).astype(jnp.bfloat16))
        both = jnp.dot(third_op_ref[which], jnp.concatenate(columns, axis=1), preferred_element_type=jnp.float32)
        for i in range(8):
            lanes = slice(i * 128, (i + 1) * 128)
            held[which * 8 + i] = jnp.where(keep, both[:64, lanes], both[64:, lanes])
        here = pl.ds(which * 8, 8)
        copies.append(pltpu.make_async_copy(held.at[here], out_ref.at[here], out_sem.at[which]))
        copies[-1].start()
    for copy in copies:
        copy.wait()


def last_contractions(rows, second_op, third_op):
    vmem = pl.BlockSpec(memory_space=pltpu.VMEM)
    return pl.pallas_call(
        contract_kernel,
        out_shape=jax.ShapeDtypeStruct((64, 64, 128), jnp.float32),
        in_specs=[vmem, vmem, vmem],
        out_specs=pl.BlockSpec(memory_space=pltpu.HBM),
        scratch_shapes=[
            pltpu.VMEM((8, 2, 256, 128), jnp.float32),
            pltpu.VMEM((64, 64, 128), jnp.float32),
            pltpu.SemaphoreType.DMA((8,)),
        ],
        compiler_params=pltpu.CompilerParams(vmem_limit_bytes=16 << 20),
    )(rows, second_op, third_op)


def on_device(eigvecs, momenta, perams, sources, spins):
    operands = first_contraction(
        eigvecs[0], jnp.transpose(momenta), sources, jnp.transpose(spins, (0, 2, 1)), perams[0]
    )
    result = last_contractions(*operands)
    result = jnp.transpose(result.reshape(64, 32, 2, 128), (0, 2, 1, 3))
    return result.reshape(1, 4, 2, 8, 2, 4096)


def solution(mesh):
    placed = (
        P("tpair", None, None, None, "space"),
        P(),
        P("tpair", None, None, None, None),
        P(),
        P(),
    )
    return jax.shard_map(
        on_device,
        mesh=mesh,
        in_specs=placed,
        out_specs=P("tpair", None, None, "space", None, None),
        check_vma=False,
    )
```

```python
import functools

import jax
import jax.numpy as jnp
from jax import lax
from jax.experimental import pallas as pl
from jax.experimental.pallas import tpu as pltpu
from jax.sharding import PartitionSpec as P

LEXT = 64
TWO_PI = 6.283185307179586
MESH = pl.DeviceIdType.MESH

NX, NZ, NC = 4, 8, 2
NY = 4
HALF = NZ // 2


def place():
    index = lax.axis_index("space")
    return lax.div(index, NZ * NC), lax.rem(lax.div(index, NC), NZ), lax.rem(index, NC)


def at_space(x, z, c):
    return {"space": (x * NZ + z) * NC + c}


def elemental_kernel(
    vec_ref, mom_hbm, sources_hbm, spins_hbm, per_ref, rows_ref, second_op_ref, third_op_ref,
    cosines, sines, fields, vfloat, left, right, total, core_in, own_sum, outbox, inbox, chunk, all_chunks,
    arrived, wide, full, first_op, mom_ref, sources_ref, spins_ref, small_sem, own_sem, ring_send, ring_recv, core_send, core_recv, sum_send, sum_recv,
    share_send, share_recv, swap_send, swap_recv, per_send, per_recv, per_own,
):
    own = pltpu.make_async_copy(vec_ref, fields.at[0], own_sem)
    own.start()
    small = [
        pltpu.make_async_copy(mom_hbm, mom_ref, small_sem.at[0]),
        pltpu.make_async_copy(sources_hbm, sources_ref, small_sem.at[1]),
        pltpu.make_async_copy(spins_hbm, spins_ref, small_sem.at[2]),
    ]
    for copy in small:
        copy.start()
    x, z, c = place()
    y = lax.axis_index("tpair")
    zhalf, zz = lax.div(z, HALF), lax.rem(z, HALF)
    slot_q = zz * NC + c
    on_right = at_space(x, lax.rem(z + 1, NZ), c)
    on_left = at_space(x, lax.rem(z + NZ - 1, NZ), c)
    partner = at_space(x, z, 1 - c)
    across = [at_space(lax.rem(x + step, NX), z, c) for step in range(1, NX)]
    along = [at_space(x, zhalf * HALF + lax.rem(zz + step, HALF), c) for step in range(1, HALF)]
    sinks = [{"tpair": lax.rem(y + step, NY)} for step in range(1, NY)]

    barrier = pltpu.get_barrier_semaphore()
    greeted = [on_right, on_left, partner] + across + along + sinks
    for target in greeted:
        pl.semaphore_signal(barrier, inc=1, device_id=target, device_id_type=MESH)
    pl.semaphore_wait(barrier, len(greeted))
    own.wait()

    def remote(source, target, send_sem, recv_sem, device):
        return pltpu.make_async_remote_copy(
            src_ref=source, dst_ref=target, send_sem=send_sem, recv_sem=recv_sem,
            device_id=device, device_id_type=MESH,
        )

    def ring_copy(rel, piece, rightward):
        there = (rel + NZ - 1) % NZ if rightward else (rel + 1) % NZ
        return remote(
            fields.at[rel, piece // 3, piece % 3], fields.at[there, piece // 3, piece % 3], ring_send, ring_recv.at[there, piece],
            on_right if rightward else on_left,
        )

    for piece in range(6):
        ring_copy(0, piece, True).start()
        ring_copy(0, (piece + 3) % 6, False).start()

    for step in range(1, NY):
        remote(per_ref.at[lax.rem(y + step, NY)], arrived.at[y], per_send, per_recv, sinks[step - 1]).start()
    per_local = pltpu.make_async_copy(per_ref.at[y], arrived.at[y], per_own)
    per_local.start()

    def relay(step, late):
        for count in range(3):
            for rightward in (True, False):
                piece = count + 3 * (late if rightward else 1 - late)
                if step == HALF and late:
                    continue
                rel = NZ - step if rightward else step
                here = fields.at[rel, piece // 3, piece % 3]
                remote(here, here, ring_send, ring_recv.at[rel, piece], on_right if rightward else on_left).wait_recv()
                if step < HALF - 1 or (step == HALF - 1 and not late):
                    ring_copy(rel, piece, rightward).start()

    for copy in small:
        copy.wait()

    row = lax.broadcasted_iota(jnp.int32, (NZ, 128), 0)
    lane = lax.broadcasted_iota(jnp.int32, (NZ, 128), 1)
    sites = ((x * NZ + ((z + row) & (NZ - 1))) * NC + c) * 128 + lane
    xs, ys, zs = sites & (LEXT - 1), (sites >> 6) & (LEXT - 1), sites >> 12
    factor = lax.rsqrt(jnp.float32(24.0 * 128 * NX * NZ * NC))
    for mom in range(4):
        mine = 2 * mom + zhalf
        turns = mom_ref[0, mine] * xs + mom_ref[1, mine] * ys + mom_ref[2, mine] * zs
        angle = (turns & (LEXT - 1)).astype(jnp.float32) * (TWO_PI / LEXT)
        cosines[mom] = jnp.cos(angle) * factor
        sines[mom] = jnp.sin(angle) * factor

    total[...] = jnp.zeros_like(total)

    def build(rel, slot):
        for part in range(2):
            for colour in range(3):
                values = fields[rel, part, colour].astype(jnp.float32)
                vfloat[part, colour, 0:64] = values
                vfloat[part, colour, 64:128] = values
        at = pl.ds(rel, 1)
        for colour in range(3):
            for odd in range(2):
                rows = pl.ds(odd, 32, stride=2)
                vr, vi = vfloat[0, colour, rows], vfloat[1, colour, rows]
                for mom in range(4):
                    cosine, sine = cosines[mom, at, :], sines[mom, at, :]
                    pr = (cosine * vr + sine * vi).astype(jnp.bfloat16)
                    pi = (cosine * vi - sine * vr).astype(jnp.bfloat16)
                    upper, lower = pl.ds(mom * 128 + odd * 32, 32), pl.ds(mom * 128 + 64 + odd * 32, 32)
                    first, second = pl.ds(colour * 128, 128), pl.ds((3 + colour) * 128, 128)
                    right[slot, upper, first] = pr
                    right[slot, upper, second] = -pi
                    right[slot, lower, first] = pi
                    right[slot, lower, second] = pr
        for colour in range(3):
            nxt, aft = (colour + 1) % 3, (colour + 2) % 3
            for odd in range(2):
                rows = pl.ds(odd, 32, stride=2)
                lrn, lin = vfloat[0, nxt, rows], vfloat[1, nxt, rows]
                lra, lia = vfloat[0, aft, rows], vfloat[1, aft, rows]
                for core in range(2):
                    for group in range(4):
                        rows = pl.ds(1 + zz * NC + core + 8 * group + odd, 32, stride=2)
                        rrn, rin = vfloat[0, nxt, rows], vfloat[1, nxt, rows]
                        rra, ria = vfloat[0, aft, rows], vfloat[1, aft, rows]
                        real = lrn * rra - lin * ria - (lra * rrn - lia * rin)
                        imag = lrn * ria + lin * rra - (lra * rin + lia * rrn)
                        where = pl.ds(core * 256 + group * 64 + odd * 32, 32)
                        left[slot, where, colour * 128 : (colour + 1) * 128] = real.astype(jnp.bfloat16)
                        left[slot, where, (3 + colour) * 128 : (4 + colour) * 128] = imag.astype(jnp.bfloat16)
    def multiply(slot):
        product = lax.dot_general(
            left[slot], right[slot], (((1,), (1,)), ((), ())), preferred_element_type=jnp.float32
        )
        for core in range(2):
            for group in range(4):
                at = core * 256 + group * 64
                for mom in range(4):
                    total[core, group, mom] += product[at : at + 64, mom * 128 : (mom + 1) * 128]

    left[1] = jnp.zeros_like(left[1])
    right[1] = jnp.zeros_like(right[1])
    schedule = ((0, 1, 0), (0, 1, 1), (1, 2, 0), (1, 2, 1), (3, 3, 0), (4, 3, 1), (6, 4, 0))

    def body(pair, carry):
        for slot in range(2):
            n = 2 * pair + slot
            build(NZ - (n + 1) // 2 if slot else n // 2, slot)
            multiply(1 - slot)
            for after, step, late in schedule:
                if after % 2 == slot:
                    pl.when(pair == after // 2)(functools.partial(relay, step, late))
        return carry

    lax.fori_loop(0, NZ // 2, body, 0)
    multiply(1)

    for group in range(4):
        remote(total.at[1 - c, group], core_in.at[group], core_send, core_recv.at[group], partner).start()

    def share_arrival(group, step):
        owner = lax.rem(zz + HALF - step, HALF) * NC + c
        return remote(
            chunk.at[group], all_chunks.at[group, owner], share_send, share_recv.at[group, step - 1], along[step - 1]
        )

    def swap_copy(group, step):
        owner = lax.rem(zz + HALF - step, HALF) * NC + c
        return remote(
            chunk.at[group] if step == 0 else all_chunks.at[group, owner],
            all_chunks.at[group, owner], swap_send, swap_recv.at[group], partner,
        )

    low = lax.broadcasted_iota(jnp.int32, (32, 128), 1) < 64
    even = lax.broadcasted_iota(jnp.int32, (32, 128), 1) % 2 == 0
    row = lax.broadcasted_iota(jnp.int32, (16, 128), 0)
    lane = lax.broadcasted_iota(jnp.int32, (16, 128), 1)
    rank = lax.axis_index("space") % 8
    pick = (lane == (row // 8) * 64 + rank * 8 + row % 8).astype(jnp.float32).astype(jnp.bfloat16)
    row = lax.broadcasted_iota(jnp.int32, (128, 128), 0)
    lane = lax.broadcasted_iota(jnp.int32, (128, 128), 1)
    wanted = (row % 2) * 64 + 2 * (row % 64 // 2) + row // 64
    order = (lane == wanted).astype(jnp.float32).astype(jnp.bfloat16)

    def rolled(value):
        return pltpu.roll(value, 64, 1)

    def tau(which, quark):
        source, comb = sources_ref[which // 2], which % 2
        spin = spins_ref[comb, 0, quark] * 4 + spins_ref[comb, 1, quark]
        flat = arrived[source, spin].astype(jnp.float32)
        for pair in range(32):
            wide[quark, 2 * pair : 2 * pair + 2, :] = flat[:, pair * 128 : (pair + 1) * 128]
        return wide[quark, pl.ds(0, 32, stride=2), :], wide[quark, pl.ds(1, 32, stride=2), :]

    def both_of_pair(value):
        turned, zero = rolled(value), jnp.zeros_like(value)
        return jnp.concatenate(
            [
                jnp.where(low, value, zero),
                jnp.where(low, turned, zero),
                jnp.where(low, zero, turned),
                jnp.where(low, zero, value),
            ],
            axis=0,
        ).astype(jnp.bfloat16)

    def arranged(upper, lower):
        uturn, lturn = rolled(upper), rolled(lower)
        straight = jnp.where(low, jnp.where(even, upper, uturn), jnp.where(even, lturn, lower))
        turned = jnp.where(low, jnp.where(even, uturn, upper), jnp.where(even, lower, lturn))
        return [straight, turned]

    def operators(which, carry):
        real, imag = tau(which, 0)
        upper = jnp.concatenate([real, rolled(real), -imag, -rolled(imag)], axis=0)
        lower = jnp.concatenate([rolled(imag), imag, rolled(real), real], axis=0)
        lanes = lax.broadcasted_iota(jnp.int32, (128, 128), 1)
        picked = lax.dot_general(
            pick,
            jnp.where(lanes < 64, upper, lower).astype(jnp.bfloat16),
            (((1,), (1,)), ((), ())),
            preferred_element_type=jnp.float32,
        )
        for part in range(2):
            at = pl.ds(pl.multiple_of(part * 64 + which * 8, 8), 8)
            first_op[at, :] = picked[part * 8 : part * 8 + 8]
        real, imag = tau(which, 2)
        second_op_ref[which, 0] = both_of_pair(real)
        second_op_ref[which, 1] = both_of_pair(imag)
        real, imag = tau(which, 1)
        operator = jnp.concatenate(arranged(real, imag) + arranged(-imag, real), axis=0)
        third_op_ref[which] = lax.dot_general(
            order, operator.astype(jnp.bfloat16), (((1,), (1,)), ((), ())),
            preferred_element_type=jnp.float32,
        ).astype(jnp.bfloat16)
        return carry

    for group in range(4):
        remote(core_in.at[group], core_in.at[group], core_send, core_recv.at[group], partner).wait_recv()
        for step in (2, 1, 3):
            mom = lax.rem(x + step, NX)
            outbox[group, step - 1] = (total[c, group, mom] + core_in[group, mom]).astype(jnp.bfloat16)
            remote(
                outbox.at[group, step - 1], inbox.at[group, step - 1], sum_send, sum_recv.at[group], across[step - 1]
            ).start()
        own_sum[group] = total[c, group, x] + core_in[group, x]

    per_local.wait()
    remote(per_ref.at[0:3], arrived.at[0:3], per_send, per_recv, sinks[0]).wait()

    for group in range(4):
        remote(inbox.at[group], inbox.at[group], sum_send, sum_recv.at[group], across[0]).wait_recv()
        summed = own_sum[group]
        for step in range(3):
            summed = summed + inbox[group, step].astype(jnp.float32)
        chunk[group] = summed.astype(jnp.bfloat16)
        for step in (3, 2, 1):
            remote(
                chunk.at[group], all_chunks.at[group, slot_q], share_send, share_recv.at[group, step - 1], along[step - 1]
            ).start()
        swap_copy(group, 0).start()
        all_chunks[group, slot_q] = chunk[group]

    lax.fori_loop(0, 8, operators, 0)
    full[pl.ds(0, 32, stride=129), :] = jnp.zeros((32, 128), jnp.float32)
    full[pl.ds(96, 32, stride=129), :] = jnp.zeros((32, 128), jnp.float32)

    def onward(group):
        for step in (1, 3, 2):
            share_arrival(group, step).wait_recv()
            swap_copy(group, step).start()

    def expand(group):
        remote(chunk, chunk, swap_send, swap_recv.at[group], partner).wait_recv()
        for q in range(8):
            d = 1 + q + 8 * group
            for odd in range(2):
                piece = all_chunks[group, q, odd * 32 : odd * 32 + 32, :].astype(jnp.float32)
                kodd = (odd + d) % 2
                e = (odd + d - kodd) // 2
                base = odd * 64 + kodd * 32 + e
                full[pl.ds(base, 32 - e, stride=129), :] = piece[: 32 - e]
                if e:
                    full[pl.ds(129 * (32 - e) + base - 32, e, stride=129), :] = piece[32 - e :]
                if d < 32:
                    base = 128 * e + kodd * 64 + odd * 32
                    full[pl.ds(base, 32 - e, stride=129), :] = -piece[: 32 - e]
                    if e:
                        full[pl.ds(129 * (32 - e) + base - 4096, e, stride=129), :] = -piece[32 - e :]

    onward(0)
    onward(1)
    expand(0)
    onward(2)
    expand(1)
    onward(3)
    expand(2)
    expand(3)

    operator = first_op[...].astype(jnp.bfloat16)
    for two in range(16):
        block = full[two * 256 : (two + 1) * 256, :].astype(jnp.bfloat16)
        first = lax.dot_general(
            operator, block, (((1,), (1,)), ((), ())), preferred_element_type=jnp.float32
        )
        for part in range(2):
            for which in range(8):
                at = part * 64 + which * 8
                piece = jnp.concatenate([first[at : at + 8, :128], first[at : at + 8, 128:]], axis=0)
                rows_ref[which, two * 16 : two * 16 + 16, part * 128 : (part + 1) * 128] = piece.astype(jnp.bfloat16)

    remote(fields.at[0:7], fields.at[0:7], ring_send, ring_recv.at[0, 0], on_right).wait_send()
    remote(core_in, core_in, core_send, core_recv.at[0], partner).wait_send()
    remote(outbox, inbox, sum_send, sum_recv.at[0], across[0]).wait_send()
    remote(outbox, inbox, share_send, share_recv.at[0, 0], along[0]).wait_send()
    remote(all_chunks.at[0:2], all_chunks.at[0:2], swap_send, swap_recv.at[0], partner).wait_send()


def first_contraction(vecs, momenta, sources, spins, perams):
    vmem = pl.BlockSpec(memory_space=pltpu.VMEM)
    hbm = pl.BlockSpec(memory_space=pltpu.HBM)
    dma, bf16, f32 = pltpu.SemaphoreType.DMA, jnp.bfloat16, jnp.float32
    return pl.pallas_call(
        elemental_kernel,
        out_shape=(
            jax.ShapeDtypeStruct((8, 256, 256), bf16),
            jax.ShapeDtypeStruct((8, 2, 128, 128), bf16),
            jax.ShapeDtypeStruct((8, 128, 128), bf16),
        ),
        in_specs=[hbm, hbm, hbm, hbm, hbm],
        out_specs=(vmem, vmem, vmem),
        scratch_shapes=[
            pltpu.VMEM((4, NZ, 128), f32),
            pltpu.VMEM((4, NZ, 128), f32),
            pltpu.VMEM((NZ, 2, 3, 64, 128), bf16),
            pltpu.VMEM((2, 3, 128, 128), f32),
            pltpu.VMEM((2, 512, 768), bf16),
            pltpu.VMEM((2, 512, 768), bf16),
            pltpu.VMEM((2, 4, 4, 64, 128), f32),
            pltpu.VMEM((4, 4, 64, 128), f32),
            pltpu.VMEM((4, 64, 128), f32),
            pltpu.VMEM((4, 3, 64, 128), bf16),
            pltpu.VMEM((4, 3, 64, 128), bf16),
            pltpu.VMEM((4, 64, 128), bf16),
            pltpu.VMEM((4, 8, 64, 128), bf16),
            pltpu.VMEM(perams.shape, bf16),
            pltpu.VMEM((3, 64, 128), f32),
            pltpu.VMEM((4096, 128), f32),
            pltpu.VMEM((128, 128), f32),
            pltpu.SMEM((3, 8), jnp.int32),
            pltpu.SMEM((4,), jnp.int32),
            pltpu.SMEM((2, 2, 3), jnp.int32),
            dma((3,)), dma(()), dma(()), dma((NZ, 6)), dma(()), dma((4,)), dma(()), dma((4,)),
            dma(()), dma((4, 3)), dma(()), dma((4,)), dma(()), dma(()), dma(()),
        ],
        compiler_params=pltpu.CompilerParams(
            collective_id=0, has_side_effects=True, vmem_limit_bytes=20 << 20
        ),
    )(*[pltpu.with_memory_space_constraint(value, pltpu.HBM) for value in (vecs, momenta, sources, spins, perams)])


def contract_kernel(rows_ref, second_op_ref, third_op_ref, out_ref, second, held, out_sem):
    keep = lax.broadcasted_iota(jnp.int32, (64, 128), 1) < 64
    copies = []
    for which in range(8):
        kreal, kimag = second_op_ref[which, 0], second_op_ref[which, 1]
        operator = jnp.concatenate(
            [jnp.concatenate([kreal, kimag], axis=1), jnp.concatenate([-kimag, kreal], axis=1)], axis=0
        )
        product = jnp.dot(rows_ref[which], operator, preferred_element_type=jnp.float32)
        for part in range(2):
            second[which, part] = product[:, part * 128 : (part + 1) * 128]
    for which in range(8):
        columns = []
        for i in range(8):
            parts = []
            for part in range(2):
                straight = second[which, part, pl.ds(i, 32, stride=8), :]
                parts += [straight, pltpu.roll(straight, 64, 1)]
            columns.append(jnp.concatenate(parts, axis=0).astype(jnp.bfloat16))
        both = jnp.dot(third_op_ref[which], jnp.concatenate(columns, axis=1), preferred_element_type=jnp.float32)
        for i in range(8):
            lanes = slice(i * 128, (i + 1) * 128)
            held[which * 8 + i] = jnp.where(keep, both[:64, lanes], both[64:, lanes])
        here = pl.ds(which * 8, 8)
        copies.append(pltpu.make_async_copy(held.at[here], out_ref.at[here], out_sem.at[which]))
        copies[-1].start()
    for copy in copies:
        copy.wait()


def last_contractions(rows, second_op, third_op):
    vmem = pl.BlockSpec(memory_space=pltpu.VMEM)
    return pl.pallas_call(
        contract_kernel,
        out_shape=jax.ShapeDtypeStruct((64, 64, 128), jnp.float32),
        in_specs=[vmem, vmem, vmem],
        out_specs=pl.BlockSpec(memory_space=pltpu.HBM),
        scratch_shapes=[
            pltpu.VMEM((8, 2, 256, 128), jnp.float32),
            pltpu.VMEM((64, 64, 128), jnp.float32),
            pltpu.SemaphoreType.DMA((8,)),
        ],
        compiler_params=pltpu.CompilerParams(vmem_limit_bytes=16 << 20),
    )(rows, second_op, third_op)


def on_device(eigvecs, momenta, perams, sources, spins):
    operands = first_contraction(
        eigvecs[0], jnp.transpose(momenta), sources, jnp.transpose(spins, (0, 2, 1)), perams[0]
    )
    result = last_contractions(*operands)
    result = jnp.transpose(result.reshape(64, 32, 2, 128), (0, 2, 1, 3))
    return result.reshape(1, 4, 2, 8, 2, 4096)


def solution(mesh):
    placed = (
        P("tpair", None, None, None, "space"),
        P(),
        P("tpair", None, None, None, None),
        P(),
        P(),
    )
    return jax.shard_map(
        on_device,
        mesh=mesh,
        in_specs=placed,
        out_specs=P("tpair", None, None, "space", None, None),
        check_vma=False,
    )
```
